256 devices in a mesh: zone: 8 (over x, z_lo), dom: 32 (over y, z_hi, core).
Axes of the slice: x: 4, y: 4, z: 8 (z_hi: 4, z_lo: 2; z = z_hi * 2 + z_lo), core: 2. Of those that a mesh axis runs over, the one named last changes fastest.
Arguments:
- state: float32 [8, 32, 5, 512], P('zone', 'dom'), as said below
- grad_op: bfloat16 [8, 32, 4, 3, 128, 384], P('zone', 'dom'), may hold values from -0.3125 to 0.3125
- adjacency: int32 [8, 32, 4, 3], P('zone', 'dom'), may hold values from 0 to 3, as said below
- node_vel: float32 [8, 32, 3, 512], P('zone', 'dom'), may hold values from -5 to 5
- face_normal: float32 [8, 32, 3, 25600], P('zone', 'dom'), as said below
- face_nodes: int32 [8, 32, 4, 25600], P('zone', 'dom'), may hold values from 0 to 767
- inner_cells: int32 [8, 32, 2, 1024], P('zone', 'dom'), may hold values from 0 to 511
- iface_cells: int32 [8, 32, 6, 4096], P('zone', 'dom'), may hold values from 0 to 511
- cell_volume: float32 [8, 32, 512], P('zone', 'dom'), may hold values from 0.5 to 2
- block_counts: int32 [8, 32], P('zone', 'dom'), may hold values from 1 to 4, as said below
Outputs:
- content: float32 [8, 32, 5, 512], P('zone', 'dom')
- new_volume: float32 [8, 32, 512], P('zone', 'dom')
The draws below stay inside these ranges and needn't reach their ends.
Inputs may be any that keep to these rules, and one draw needn't show every extreme that they name: `state`: density 0.5 to 2, velocity components -0.3 to 0.3 and pressure 1 to 2 in every cell, stored as conserved variables. `adjacency`: entry 0 of each block's stencil is the block itself. `face_normal`: every area vector has length 0.5 to 1.5. `block_counts`: at least one partition has all 4 blocks live.
All inputs are finite; a program needn't handle non-finite values.
Results may differ from the reference program's by a relative error of at most 0.00054.
Values sent between devices are 32-bit elements; how exact they have to be, the bound alone decides.
A program may use at most 128 MiB of HBM per device.

```python
import math
import jax
import jax.numpy as jnp
import numpy as np
from jax import lax

CB = 128
NB = 4
K = 3
FB = 32
ROUNDS = 6
HN = 128
NN = 512
NIN = 1024
FACES = 25600
N_ZONE = 8
N_DOM = 32


def draw_state(key, part):
    key_list = jax.random.split(jax.random.fold_in(key, 11), 3)
    cell_shape = (N_ZONE, N_DOM, NB * CB)
    density = jax.random.uniform(key_list[0], cell_shape, jnp.float32, 0.5, 2.0)
    velocity = jax.random.uniform(key_list[1], (3,) + cell_shape, jnp.float32, -0.3, 0.3)
    pressure = jax.random.uniform(key_list[2], cell_shape, jnp.float32, 1.0, 2.0)
    energy = pressure / 0.4 + 0.5 * density * jnp.sum(velocity * velocity, axis=0)
    momentum = density[None] * velocity
    return jnp.stack([density, momentum[0], momentum[1], momentum[2], energy], axis=2)


def draw_adjacency(key, part):
    chosen = jax.random.randint(jax.random.fold_in(key, 12), (N_ZONE, N_DOM, NB, K), 0, NB)
    itself = jnp.broadcast_to(jnp.arange(NB, dtype=jnp.int32)[:, None], (N_ZONE, N_DOM, NB, 1))
    return jnp.concatenate([itself, chosen[..., 1:]], axis=3).astype(jnp.int32)


def draw_face_normal(key, part):
    key_list = jax.random.split(jax.random.fold_in(key, 13), 3)
    face_shape = (N_ZONE, N_DOM, FACES)
    height = jax.random.uniform(key_list[0], face_shape, jnp.float32, -1.0, 1.0)
    azimuth = jax.random.uniform(key_list[1], face_shape, jnp.float32, -jnp.pi, jnp.pi)
    face_area = jnp.exp(jax.random.uniform(key_list[2], face_shape, jnp.float32, jnp.log(0.5), jnp.log(1.5)))
    radial = jnp.sqrt(jnp.maximum(1.0 - height * height, 0.0))
    return jnp.stack([face_area * radial * jnp.cos(azimuth), face_area * radial * jnp.sin(azimuth), face_area * height], axis=2)


def draw_block_counts(key, part):
    key_list = jax.random.split(jax.random.fold_in(key, 14), 2)
    partial_counts = jax.random.randint(key_list[0], (N_ZONE, N_DOM), 1, max(2, NB // 2) + 1)
    full_ones = jax.random.randint(key_list[1], (N_ZONE, N_DOM), 0, 4) == 0
    counts = jnp.where(full_ones, NB, partial_counts)
    return counts.at[0, 0].set(NB).astype(jnp.int32)


def place_ends(values, rng, least, top_value):
    place = [jax.random.randint(jax.random.fold_in(rng, axis), (), 0, length) for axis, length in enumerate(values.shape)]
    longest = values.shape.index(max(values.shape))
    neighbour = place[:longest] + [(place[longest] + 1) % values.shape[longest]] + place[longest + 1:]
    return values.at[tuple(place)].set(least).at[tuple(neighbour)].set(top_value)


def steps_of(key, shape, cuts, smallest, high):
    def one(dim, blocks):
        draws = jax.random.uniform(jax.random.fold_in(jax.random.fold_in(key, 6), dim), (blocks,), jnp.float32, smallest / len(cuts), high / len(cuts))
        return jnp.repeat(jnp.exp(draws), shape[dim] // blocks).reshape((-1,) + (1,) * (len(shape) - dim - 1))

    gain = one(*cuts[0])
    for cut in cuts[1:]:
        gain = gain * one(*cut)
    return gain


def normal_values(rng, shape, deviation, reach, cuts=(), kind=jnp.bfloat16):
    values = deviation * jax.random.normal(rng, shape, jnp.float32)
    if cuts:
        values = values * steps_of(rng, shape, cuts, -0.22, 0.18)
    return jnp.clip(values, -reach, reach).astype(kind)


def setup_inputs(seed: int = 0) -> dict:
    key_of = jax.random.split(jax.random.key(seed), 11)
    state = draw_state(jax.random.fold_in(key_of[10], 71), 0)
    grad_op = normal_values(key_of[1], (N_ZONE, N_DOM, NB, K, CB, 3 * CB), (K * CB) ** -0.5, 0.3125, ((0, 8), (1, 32)))
    adjacency = draw_adjacency(jax.random.fold_in(key_of[10], 71), 0)
    node_vel = normal_values(key_of[3], (N_ZONE, N_DOM, 3, NN), 1.0, 5.0, ((0, 8), (1, 32)), jnp.float32)
    face_normal = draw_face_normal(jax.random.fold_in(key_of[10], 71), 0)
    face_nodes = place_ends(jax.random.randint(key_of[5], (N_ZONE, N_DOM, 4, FACES), 0, NN + 2 * HN), jax.random.fold_in(key_of[5], 1), 0, (NN + 2 * HN) - 1).astype(jnp.int32)
    inner_cells = place_ends(jax.random.randint(key_of[6], (N_ZONE, N_DOM, 2, NIN), 0, NN), jax.random.fold_in(key_of[6], 1), 0, NN - 1).astype(jnp.int32)
    iface_cells = place_ends(jax.random.randint(key_of[7], (N_ZONE, N_DOM, ROUNDS, FB * CB), 0, NN), jax.random.fold_in(key_of[7], 1), 0, NN - 1).astype(jnp.int32)
    cell_volume = jnp.clip(jnp.exp(math.log(2.0) - 1.3862944 * jax.random.uniform(key_of[8], (N_ZONE, N_DOM, NN), jnp.float32) ** steps_of(key_of[8], (N_ZONE, N_DOM, NN), ((0, 8), (1, 32)), -0.2, 0.2)), 0.5, 2.0)
    block_counts = draw_block_counts(jax.random.fold_in(key_of[10], 71), 0)
    return dict(state=state, grad_op=grad_op, adjacency=adjacency, node_vel=node_vel, face_normal=face_normal, face_nodes=face_nodes, inner_cells=inner_cells, iface_cells=iface_cells, cell_volume=cell_volume, block_counts=block_counts)


GAMMA_LESS = 0.4
STEP_SIZE = 0.25
RECON_GAIN = 0.2
FIX_SHARE = 0.1

def primitives(face_states):
    density = face_states[0]
    velocity = face_states[1:4] / density
    pressure = GAMMA_LESS * (face_states[4] - 0.5 * density * lax.optimization_barrier(jnp.sum(velocity * velocity, axis=0)))
    enthalpy = (face_states[4] + pressure) / density
    return (density, velocity, pressure, enthalpy)

def rebuild(values, slopes, normal):
    delta = lax.optimization_barrier(jnp.sum(slopes * normal[None], axis=1))
    density = values[0]
    energy = values[4]
    new_density = density * (1.0 + RECON_GAIN * jnp.tanh(delta[0] / density))
    new_momentum = values[1:4] + RECON_GAIN * density * jnp.tanh(delta[1:4] / density)
    new_energy = energy * (1.0 + RECON_GAIN * jnp.tanh(delta[4] / energy))
    return jnp.concatenate([new_density[None], new_momentum, new_energy[None]], axis=0)

def physical(face_states, velocity, pressure, unit_normal, grid_speed):
    normal_speed = lax.optimization_barrier(jnp.sum(velocity * unit_normal, axis=0))
    moving = normal_speed - grid_speed
    mass_flux = face_states[0] * moving
    momentum = face_states[1:4] * moving + pressure * unit_normal
    energy = face_states[4] * moving + pressure * normal_speed
    return jnp.concatenate([mass_flux[None], momentum, energy[None]], axis=0)

def roe_flux(left_side, right_side, normal, sweeps):
    face_area = jnp.sqrt(lax.optimization_barrier(jnp.sum(normal * normal, axis=0)))
    unit_normal = normal / face_area
    grid_speed = sweeps / (STEP_SIZE * face_area)
    dens_left, vel_left, pres_left, enth_left = primitives(left_side)
    dens_right, vel_right, pres_right, enth_right = primitives(right_side)
    root_left = jnp.sqrt(dens_left)
    root_right = jnp.sqrt(dens_right)
    weight_sum = root_left + root_right
    mean_vel = (root_left * vel_left + root_right * vel_right) / weight_sum
    mean_enth = (root_left * enth_left + root_right * enth_right) / weight_sum
    mean_dens = root_left * root_right
    mean_normal = lax.optimization_barrier(jnp.sum(mean_vel * unit_normal, axis=0))
    kinetic = 0.5 * lax.optimization_barrier(jnp.sum(mean_vel * mean_vel, axis=0))
    sound_speed = jnp.sqrt(GAMMA_LESS * (mean_enth - kinetic))
    sound_sq = sound_speed * sound_speed
    jump_pres = pres_right - pres_left
    jump_dens = dens_right - dens_left
    jump_vel = vel_right - vel_left
    jump_normal = lax.optimization_barrier(jnp.sum(jump_vel * unit_normal, axis=0))
    entropy_fix = (FIX_SHARE * sound_speed) ** 2
    wave_slow = jnp.sqrt((mean_normal - sound_speed - grid_speed) ** 2 + entropy_fix)
    wave_mid = jnp.sqrt((mean_normal - grid_speed) ** 2 + entropy_fix)
    wave_fast = jnp.sqrt((mean_normal + sound_speed - grid_speed) ** 2 + entropy_fix)
    amp_slow = (jump_pres - mean_dens * sound_speed * jump_normal) / (2.0 * sound_sq)
    amp_fast = (jump_pres + mean_dens * sound_speed * jump_normal) / (2.0 * sound_sq)
    amp_mid = jump_dens - jump_pres / sound_sq
    shear = jump_vel - jump_normal * unit_normal
    slow_part = wave_slow * amp_slow
    fast_part = wave_fast * amp_fast
    diss_mass = slow_part + wave_mid * amp_mid + fast_part
    diss_mom = slow_part * (mean_vel - sound_speed * unit_normal) + wave_mid * (amp_mid * mean_vel + mean_dens * shear) + fast_part * (mean_vel + sound_speed * unit_normal)
    diss_energy = slow_part * (mean_enth - sound_speed * mean_normal) + wave_mid * (amp_mid * kinetic + mean_dens * (lax.optimization_barrier(jnp.sum(mean_vel * jump_vel, axis=0)) - mean_normal * jump_normal)) + fast_part * (mean_enth + sound_speed * mean_normal)
    dissipation = jnp.concatenate([diss_mass[None], diss_mom, diss_energy[None]], axis=0)
    central = physical(left_side, vel_left, pres_left, unit_normal, grid_speed) + physical(right_side, vel_right, pres_right, unit_normal, grid_speed)
    return face_area * 0.5 * (central - dissipation)

def cell_slopes(values, grad_blocks, neighbours):
    nblocks = neighbours.shape[0]
    blocks = values.astype(jnp.bfloat16).reshape(5, nblocks, CB)
    nearby = blocks[:, neighbours]
    products = jnp.einsum('vbkj,bkjc->vbc', nearby.astype(jnp.float32), grad_blocks.astype(jnp.float32), precision=lax.Precision.HIGHEST)
    return products.reshape(5, nblocks, 3, CB).transpose(0, 2, 1, 3).reshape(5, 3, nblocks * CB)

def swept_volumes(extended, node_lists, normal):
    mean_vel = 0.25 * (extended[:, node_lists[0]] + extended[:, node_lists[1]] + extended[:, node_lists[2]] + extended[:, node_lists[3]])
    return STEP_SIZE * lax.optimization_barrier(jnp.sum(normal * mean_vel, axis=0))

def interior_terms(values, slopes, normal, sweeps, cell_pairs):
    count_inner = cell_pairs.shape[1]
    inner_normal = normal[:, :count_inner]
    inner_sweeps = sweeps[:count_inner]
    left_cells = cell_pairs[0]
    right_cells = cell_pairs[1]
    left_side = rebuild(values[:, left_cells], slopes[:, :, left_cells], inner_normal)
    right_side = rebuild(values[:, right_cells], slopes[:, :, right_cells], -inner_normal)
    face_flux = roe_flux(left_side, right_side, inner_normal, inner_sweeps)
    residual = jnp.zeros(values.shape, jnp.float32).at[:, left_cells].add(-face_flux).at[:, right_cells].add(face_flux)
    change = jnp.zeros((values.shape[1],), jnp.float32).at[left_cells].add(inner_sweeps).at[right_cells].add(-inner_sweeps)
    return (residual, change)

def own_states(values, slopes, normal, face_cells, first_face):
    slot_count = face_cells.shape[1]
    rebuilt = []
    for round_index in range(face_cells.shape[0]):
        first_slot = first_face + round_index * slot_count
        chosen = face_cells[round_index]
        rebuilt.append(rebuild(values[:, chosen], slopes[:, :, chosen], normal[:, first_slot:first_slot + slot_count]))
    return jnp.stack(rebuilt)

def interface_terms(residual, change, own_faces, theirs, normal, sweeps, face_cells, first_face):
    slot_count = face_cells.shape[1]
    for round_index in range(face_cells.shape[0]):
        first_slot = first_face + round_index * slot_count
        seg_normal = normal[:, first_slot:first_slot + slot_count]
        seg_sweeps = sweeps[first_slot:first_slot + slot_count]
        face_flux = roe_flux(own_faces[round_index], theirs[round_index], seg_normal, seg_sweeps)
        chosen = face_cells[round_index]
        residual = residual.at[:, chosen].add(-face_flux)
        change = change.at[chosen].add(seg_sweeps)
    return (residual, change)

def reference(state, grad_op, adjacency, node_vel, face_normal, face_nodes, inner_cells, iface_cells, cell_volume, block_counts):
    devices = N_ZONE * N_DOM
    padded = jnp.pad(node_vel, ((0, 0), (1, 1), (0, 0), (0, 0)))
    extended = jnp.concatenate([padded[:, :-2, :, NN - HN:], node_vel, padded[:, 2:, :, :HN]], axis=3)
    flat_values = state.reshape((devices,) + state.shape[2:])
    flat_ops = grad_op.reshape((devices,) + grad_op.shape[2:])
    flat_adj = adjacency.reshape((devices,) + adjacency.shape[2:])
    flat_ext = extended.reshape((devices,) + extended.shape[2:])
    flat_normal = face_normal.reshape((devices,) + face_normal.shape[2:])
    flat_nodes = face_nodes.reshape((devices,) + face_nodes.shape[2:])
    flat_pairs = inner_cells.reshape((devices,) + inner_cells.shape[2:])
    flat_cells = iface_cells.reshape((devices,) + iface_cells.shape[2:])

    def first_pass(pieces):
        values, grad_blocks, neighbours, ext_nodes, normal, node_lists, cell_pairs, face_cells = pieces
        slopes = cell_slopes(values, grad_blocks, neighbours)
        sweeps = swept_volumes(ext_nodes, node_lists, normal)
        residual, change = interior_terms(values, slopes, normal, sweeps, cell_pairs)
        own_faces = own_states(values, slopes, normal, face_cells, cell_pairs.shape[1])
        return (residual, change, own_faces)
    residual, change, own_faces = lax.map(first_pass, (flat_values, flat_ops, flat_adj, flat_ext, flat_normal, flat_nodes, flat_pairs, flat_cells))
    device_list = np.arange(devices)
    partner_bits = [1, 2, 4, 8, N_DOM, 16]
    theirs = jnp.stack([own_faces[device_list ^ partner_bits[round_index], round_index] for round_index in range(ROUNDS)], axis=1)

    def second_pass(pieces):
        residual_dev, change_dev, own_dev, theirs_dev, ext_nodes, normal, node_lists, face_cells, cell_pairs = pieces
        sweeps = swept_volumes(ext_nodes, node_lists, normal)
        return interface_terms(residual_dev, change_dev, own_dev, theirs_dev, normal, sweeps, face_cells, cell_pairs.shape[1])
    residual, change = lax.map(second_pass, (residual, change, own_faces, theirs, flat_ext, flat_normal, flat_nodes, flat_cells, flat_pairs))
    residual = residual.reshape(state.shape)
    change = change.reshape(cell_volume.shape)
    live_cells = jnp.arange(NN)[None, None, :] // CB < block_counts[:, :, None]
    content = cell_volume[:, :, None, :] * state + jnp.where(live_cells[:, :, None, :], STEP_SIZE * residual, 0.0)
    new_volume = cell_volume + jnp.where(live_cells, change, 0.0)
    return (content, new_volume)
```

```python
import functools

import jax
import jax.numpy as jnp
from jax import lax
from jax.experimental import pallas as pl
from jax.experimental.pallas import tpu as pltpu
from jax.sharding import PartitionSpec as P

CB = 128
NB = 4
K = 3
ROUNDS = 6
HN = 128
NN = 512
RT = 4
TILES = 25
RS = 56

STEP_SIZE = 0.25
RECON_GAIN = 0.2
GAMMA_LESS = 0.4

SEND_ORDER = (2, 1, 5, 4, 3, 0)
FLUX_ORDER = (2, 1, 5, 4, 3, 0)

F32 = jnp.float32
BF16 = jnp.bfloat16


def take(row, lanes):
    return jnp.take_along_axis(row, lanes, axis=1, mode="promise_in_bounds")


def rows8(tile):
    return pl.ds(pl.multiple_of(tile * 8, 8), 8)


def split_cells(cells):
    return cells & 127, (cells & 128) != 0, (cells & 256) != 0


def pick(table, first, where):
    lanes, odd, upper = where
    low = jnp.where(odd, take(table[first + 1], lanes), take(table[first], lanes))
    high = jnp.where(odd, take(table[first + 3], lanes), take(table[first + 2], lanes))
    return jnp.where(upper, high, low)


def rebuild(table, where, normal):
    cons = [pick(table, 4 * v, where) for v in range(5)]
    delta = []
    for v in range(5):
        parts = [pick(table, 20 + 4 * (3 * v + d), where) * normal[d] for d in range(3)]
        delta.append(parts[0] + parts[1] + parts[2])
    per_dens = 1.0 / cons[0]
    gain = RECON_GAIN * cons[0]
    out = [cons[0] + gain * jnp.tanh(delta[0] * per_dens)]
    for v in range(1, 4):
        out.append(cons[v] + gain * jnp.tanh(delta[v] * per_dens))
    out.append(cons[4] + RECON_GAIN * cons[4] * jnp.tanh(delta[4] / cons[4]))
    return out


def dot3(a, b):
    return a[0] * b[0] + a[1] * b[1] + a[2] * b[2]


def side_values(cons, unit):
    per_dens = 1.0 / cons[0]
    vel = [cons[i] * per_dens for i in (1, 2, 3)]
    pres = GAMMA_LESS * (cons[4] - 0.5 * dot3(cons[1:4], vel))
    enth = (cons[4] + pres) * per_dens
    return vel, pres, enth, dot3(vel, unit)


def roe_flux(left, right, normal, sweep):
    area_sq = dot3(normal, normal)
    per_area = lax.rsqrt(area_sq)
    area = area_sq * per_area
    unit = [x * per_area for x in normal]
    grid = sweep * per_area * (1.0 / STEP_SIZE)
    vel_l, pres_l, enth_l, q_l = side_values(left, unit)
    vel_r, pres_r, enth_r, q_r = side_values(right, unit)
    root_l = jnp.sqrt(left[0])
    root_r = jnp.sqrt(right[0])
    per_sum = 1.0 / (root_l + root_r)
    a = root_l * per_sum
    b = root_r * per_sum
    vel = [a * x + b * y for x, y in zip(vel_l, vel_r)]
    enth = a * enth_l + b * enth_r
    dens = root_l * root_r
    q = dot3(vel, unit)
    kinetic = 0.5 * dot3(vel, vel)
    c_sq = GAMMA_LESS * (enth - kinetic)
    c = jnp.sqrt(c_sq)
    per_c_sq = 1.0 / c_sq
    d_pres = pres_r - pres_l
    d_dens = right[0] - left[0]
    d_vel = [y - x for x, y in zip(vel_l, vel_r)]
    d_q = dot3(d_vel, unit)
    fix = 0.01 * c_sq
    rel = q - grid
    slow = rel - c
    fast = rel + c
    wave_slow = jnp.sqrt(slow * slow + fix)
    wave_mid = jnp.sqrt(rel * rel + fix)
    wave_fast = jnp.sqrt(fast * fast + fix)
    half = 0.5 * per_c_sq
    cross = dens * c * d_q
    part_slow = wave_slow * ((d_pres - cross) * half)
    part_fast = wave_fast * ((d_pres + cross) * half)
    part_mid = wave_mid * (d_dens - d_pres * per_c_sq)
    shear = wave_mid * dens
    both = part_slow + part_fast
    total = both + part_mid
    diff = c * (part_fast - part_slow)
    move_l = q_l - grid
    move_r = q_r - grid
    along = pres_l + pres_r - diff + shear * d_q
    out = [left[0] * move_l + right[0] * move_r - total]
    for i in range(3):
        out.append(
            left[i + 1] * move_l
            + right[i + 1] * move_r
            + along * unit[i]
            - total * vel[i]
            - shear * d_vel[i]
        )
    out.append(
        left[4] * move_l
        + right[4] * move_r
        + pres_l * q_l
        + pres_r * q_r
        - both * enth
        - diff * q
        - part_mid * kinetic
        - shear * (dot3(vel, d_vel) - q * d_q)
    )
    scale = 0.5 * area
    return [scale * x for x in out]


def scatter(terms, where_cells, masked, total):
    lanes = where_cells & 127
    chunk = where_cells >> 7
    for v, x in enumerate(terms):
        upper = x.astype(BF16).astype(F32)
        for piece, part in enumerate((upper, x - upper)):
            for h in range(4):
                masked[pl.ds(h * 12 + piece * 6 + v, 8, stride=RS), :] = jnp.where(chunk == h, part, 0.0)
    slot = lax.broadcasted_iota(jnp.int32, (128, 128), 0)
    result = None
    for s in range(0, 8, 2):
        pair = (s, s + 1)
        left = jnp.concatenate([masked[i * RS : i * RS + 48, :].astype(BF16) for i in pair], axis=1)
        right = jnp.concatenate(
            [jnp.where(lanes[i : i + 1, :] == slot, 1.0, 0.0).astype(BF16) for i in pair], axis=1
        )
        part = lax.dot_general(left, right, (((1,), (1,)), ((), ())), preferred_element_type=F32)
        result = part if result is None else result + part
    total[...] += result


def kernel(
    remote,
    state,
    grad,
    adjacency,
    node_vel,
    face_normal,
    face_nodes,
    inner_cells,
    iface_cells,
    volume,
    counts,
    content,
    new_volume,
    table,
    nodes,
    normals,
    lists,
    pairs,
    cells,
    own,
    theirs,
    sweeps,
    halo,
    masked,
    total,
    send_sem,
    recv_sem,
    halo_send,
    halo_recv,
):
    if remote:
        zone = lax.axis_index("zone")
        dom = lax.axis_index("dom")
        n_dom = lax.axis_size("dom")
        nxt = lax.rem(dom + 1, n_dom)
        prv = lax.rem(dom + n_dom - 1, n_dom)

        def flip(at, bit):
            return at + bit * (1 - 2 * ((at // bit) % 2))

        peers = [
            (zone, flip(dom, 1)),
            (zone, flip(dom, 2)),
            (zone, flip(dom, 4)),
            (zone, flip(dom, 8)),
            (flip(zone, 1), dom),
            (zone, flip(dom, 16)),
        ]
        barrier = pltpu.get_barrier_semaphore()
        for peer in peers + [(zone, nxt), (zone, prv)]:
            pl.semaphore_signal(barrier, inc=1, device_id=peer, device_id_type=pl.DeviceIdType.MESH)

    def exchange(index):
        if remote:
            return pltpu.make_async_remote_copy(
                src_ref=own.at[index],
                dst_ref=theirs.at[index],
                send_sem=send_sem.at[index],
                recv_sem=recv_sem.at[index],
                device_id=peers[index],
                device_id_type=pl.DeviceIdType.MESH,
            )
        return pltpu.make_async_copy(own.at[index], theirs.at[index], recv_sem.at[index])

    def halo_copy(side):
        source = node_vel.at[:, pl.ds((NN - HN) * (1 - side), HN)]
        if remote:
            return pltpu.make_async_remote_copy(
                src_ref=source,
                dst_ref=halo.at[side],
                send_sem=halo_send.at[side],
                recv_sem=halo_recv.at[side],
                device_id=(zone, prv if side else nxt),
                device_id_type=pl.DeviceIdType.MESH,
            )
        return pltpu.make_async_copy(source, halo.at[side], halo_recv.at[side])

    for v in range(5):
        for h in range(4):
            table[4 * v + h] = jnp.broadcast_to(state[v : v + 1, h * CB : (h + 1) * CB], (8, CB))
    for b in range(NB):
        sums = None
        for k in range(K):
            near = jnp.full((5, CB), adjacency[b, k], jnp.int32)
            block = state[:, 0:CB]
            for other in range(1, NB):
                block = jnp.where(near == other, state[:, other * CB : (other + 1) * CB], block)
            part = jnp.dot(block.astype(BF16), grad[b, k], preferred_element_type=F32)
            sums = part if sums is None else sums + part
        for v in range(5):
            for d in range(3):
                table[20 + 4 * (3 * v + d) + b] = jnp.broadcast_to(
                    sums[v : v + 1, d * CB : (d + 1) * CB], (8, CB)
                )

    def spread(chunk, _):
        at = pl.ds(pl.multiple_of(chunk * CB, CB), CB)
        normals[pl.ds(chunk * 4, 3), :] = face_normal[:, at]
        return 0

    lax.fori_loop(0, TILES * 8, spread, 0, unroll=8)

    def spread_cells(chunk, _):
        at = pl.ds(pl.multiple_of(chunk * CB, CB), CB)
        cells[pl.ds(pl.multiple_of(chunk * 8, 8), ROUNDS), :] = iface_cells[:, at]
        return 0

    lax.fori_loop(0, RT * 8, spread_cells, 0, unroll=8)

    def normal_of(tile):
        return [normals[pl.ds(tile * 32 + d, 8, stride=4), :] for d in range(3)]

    def cells_of(index, t):
        return cells[pl.ds(t * 64 + index, 8, stride=8), :]

    if remote:
        pl.semaphore_wait(barrier, len(peers) + 2)
    for side in range(2):
        halo_copy(side).start()

    for index in SEND_ORDER:

        def own_tile(t, _, index=index):
            where = split_cells(cells_of(index, t))
            out = rebuild(table, where, normal_of(1 + RT * index + t))
            for v in range(5):
                own[index, v, rows8(t), :] = out[v]
            return 0

        lax.fori_loop(0, RT, own_tile, 0, unroll=2)
        exchange(index).start()

    def spread_lists(chunk, _):
        at = pl.ds(pl.multiple_of(chunk * CB, CB), CB)
        lists[pl.ds(chunk * 4, 4), :] = face_nodes[:, at]
        return 0

    lax.fori_loop(0, TILES * 8, spread_lists, 0, unroll=8)

    for chunk in range(8):
        pairs[pl.ds(chunk * 2, 2), :] = inner_cells[:, chunk * CB : (chunk + 1) * CB]

    for d in range(3):
        for h in range(4):
            nodes[6 * d + 1 + h] = jnp.broadcast_to(node_vel[d : d + 1, h * CB : (h + 1) * CB], (8, CB))
    for side in range(2):
        halo_copy(side).wait()
        if remote:
            inside = (dom != n_dom - 1) if side else (dom != 0)
        for d in range(3):
            row = jnp.broadcast_to(halo[side, d : d + 1, :], (8, CB))
            if remote:
                row = jnp.where(inside, row, 0.0)
            nodes[6 * d + 5 * side] = row

    def sweep_tile(tile, _):
        normal = normal_of(tile)
        sums = [None] * 3
        for corner in range(4):
            at = lists[pl.ds(tile * 32 + corner, 8, stride=4), :]
            lanes = at & 127
            chunk = at >> 7
            for d in range(3):
                value = take(nodes[6 * d], lanes)
                for h in range(1, 6):
                    value = jnp.where(chunk == h, take(nodes[6 * d + h], lanes), value)
                sums[d] = value if corner == 0 else sums[d] + value
        sweeps[rows8(tile), :] = (0.25 * STEP_SIZE) * dot3(normal, sums)
        return 0

    lax.fori_loop(0, TILES, sweep_tile, 0)

    total[...] = jnp.zeros_like(total)

    normal = normal_of(0)
    sweep = sweeps[0:8, :]
    left_cells = pairs[pl.ds(0, 8, stride=2), :]
    right_cells = pairs[pl.ds(1, 8, stride=2), :]
    left = rebuild(table, split_cells(left_cells), normal)
    right = rebuild(table, split_cells(right_cells), [-x for x in normal])
    flux = roe_flux(left, right, normal, sweep)
    scatter([-x for x in flux] + [sweep], left_cells, masked.at[0], total)
    scatter(flux + [-sweep], right_cells, masked.at[1], total)

    for index in FLUX_ORDER:
        exchange(index).wait()

        def flux_tile(t, half, index=index):
            tile = 1 + RT * index + t
            ours = [own[index, v, rows8(t), :] for v in range(5)]
            other = [theirs[index, v, rows8(t), :] for v in range(5)]
            sweep = sweeps[rows8(tile), :]
            flux = roe_flux(ours, other, normal_of(tile), sweep)
            scatter([-x for x in flux] + [sweep], cells_of(index, t), masked.at[half], total)

        def flux_pair(t, _):
            flux_tile(2 * t, 0)
            flux_tile(2 * t + 1, 1)
            return 0

        lax.fori_loop(0, RT // 2, flux_pair, 0)

    live = counts[0, 0]
    for h in range(4):
        on = jnp.full((8, CB), h, jnp.int32) < live
        at = pl.ds(h * CB, CB)
        sums = total[h * 12 : h * 12 + 6, :] + total[h * 12 + 6 : h * 12 + 12, :]
        room = volume[0:1, at]
        content[:, at] = room * state[:, at] + jnp.where(on[0:5], STEP_SIZE * sums[0:5, :], 0.0)
        new_volume[0:1, at] = room + jnp.where(on[0:1], sums[5:6, :], 0.0)


def section(remote, state, grad, adjacency, node_vel, face_normal, face_nodes, inner_cells, iface_cells, volume, counts):
    vmem = pl.BlockSpec(memory_space=pltpu.VMEM)
    smem = pl.BlockSpec(memory_space=pltpu.SMEM)
    params = dict(vmem_limit_bytes=60 << 20)
    if remote:
        params.update(collective_id=0, has_side_effects=True)
    return pl.pallas_call(
        functools.partial(kernel, remote),
        out_shape=(
            jax.ShapeDtypeStruct((5, NN), F32),
            jax.ShapeDtypeStruct((1, NN), F32),
        ),
        in_specs=[vmem, vmem, smem, vmem, vmem, vmem, vmem, vmem, vmem, smem],
        out_specs=(vmem, vmem),
        scratch_shapes=[
            pltpu.VMEM((80, 8, CB), F32),
            pltpu.VMEM((18, 8, CB), F32),
            pltpu.VMEM((TILES * 32, CB), F32),
            pltpu.VMEM((TILES * 32, CB), jnp.int32),
            pltpu.VMEM((16, CB), jnp.int32),
            pltpu.VMEM((RT * 64, CB), jnp.int32),
            pltpu.VMEM((ROUNDS, 5, RT * 8, CB), F32),
            pltpu.VMEM((ROUNDS, 5, RT * 8, CB), F32),
            pltpu.VMEM((TILES * 8, CB), F32),
            pltpu.VMEM((2, 3, HN), F32),
            pltpu.VMEM((2, 8 * RS, CB), F32),
            pltpu.VMEM((48, CB), F32),
            pltpu.SemaphoreType.DMA((ROUNDS,)),
            pltpu.SemaphoreType.DMA((ROUNDS,)),
            pltpu.SemaphoreType.DMA((2,)),
            pltpu.SemaphoreType.DMA((2,)),
        ],
        compiler_params=pltpu.CompilerParams(**params),
    )(state, grad, adjacency, node_vel, face_normal, face_nodes, inner_cells, iface_cells, volume, counts)


def shards(
    state,
    grad_op,
    adjacency,
    node_vel,
    face_normal,
    face_nodes,
    inner_cells,
    iface_cells,
    cell_volume,
    block_counts,
):
    content, new_volume = section(
        True,
        state[0, 0],
        grad_op[0, 0],
        adjacency[0, 0],
        node_vel[0, 0],
        face_normal[0, 0],
        face_nodes[0, 0],
        inner_cells[0, 0],
        iface_cells[0, 0],
        cell_volume[0],
        block_counts,
    )
    return (content[None, None], new_volume[None])


def solution(mesh):
    return jax.shard_map(
        shards,
        mesh=mesh,
        in_specs=(
            P("zone", "dom", None, None),
            P("zone", "dom", None, None, None, None),
            P("zone", "dom", None, None),
            P("zone", "dom", None, None),
            P("zone", "dom", None, None),
            P("zone", "dom", None, None),
            P("zone", "dom", None, None),
            P("zone", "dom", None, None),
            P("zone", "dom", None),
            P("zone", "dom"),
        ),
        out_specs=(P("zone", "dom", None, None), P("zone", "dom", None)),
        check_vma=False,
    )
```

```python
import functools

import jax
import jax.numpy as jnp
from jax import lax
from jax.experimental import pallas as pl
from jax.experimental.pallas import tpu as pltpu
from jax.sharding import PartitionSpec as P

CB = 128
NB = 4
K = 3
ROUNDS = 6
HN = 128
NN = 512
RT = 4
TILES = 25
RS = 56

STEP_SIZE = 0.25
RECON_GAIN = 0.2
GAMMA_LESS = 0.4

SEND_ORDER = (2, 1, 5, 4, 3, 0)
FLUX_ORDER = (2, 1, 5, 4, 3, 0)

F32 = jnp.float32
BF16 = jnp.bfloat16


def take(row, lanes):
    return jnp.take_along_axis(row, lanes, axis=1, mode="promise_in_bounds")


def rows8(tile):
    return pl.ds(pl.multiple_of(tile * 8, 8), 8)


def split_cells(cells):
    return cells & 127, (cells & 128) != 0, (cells & 256) != 0


def pick(table, first, where):
    lanes, odd, upper = where
    low = jnp.where(odd, take(table[first + 1], lanes), take(table[first], lanes))
    high = jnp.where(odd, take(table[first + 3], lanes), take(table[first + 2], lanes))
    return jnp.where(upper, high, low)


def rebuild(table, where, normal):
    cons = [pick(table, 4 * v, where) for v in range(5)]
    delta = []
    for v in range(5):
        parts = [pick(table, 20 + 4 * (3 * v + d), where) * normal[d] for d in range(3)]
        delta.append(parts[0] + parts[1] + parts[2])
    per_dens = 1.0 / cons[0]
    gain = RECON_GAIN * cons[0]
    out = [cons[0] + gain * jnp.tanh(delta[0] * per_dens)]
    for v in range(1, 4):
        out.append(cons[v] + gain * jnp.tanh(delta[v] * per_dens))
    out.append(cons[4] + RECON_GAIN * cons[4] * jnp.tanh(delta[4] / cons[4]))
    return out


def dot3(a, b):
    return a[0] * b[0] + a[1] * b[1] + a[2] * b[2]


def side_values(cons, unit):
    per_dens = 1.0 / cons[0]
    vel = [cons[i] * per_dens for i in (1, 2, 3)]
    pres = GAMMA_LESS * (cons[4] - 0.5 * dot3(cons[1:4], vel))
    enth = (cons[4] + pres) * per_dens
    return vel, pres, enth, dot3(vel, unit)


def roe_flux(left, right, normal, sweep):
    area_sq = dot3(normal, normal)
    per_area = lax.rsqrt(area_sq)
    area = area_sq * per_area
    unit = [x * per_area for x in normal]
    grid = sweep * per_area * (1.0 / STEP_SIZE)
    vel_l, pres_l, enth_l, q_l = side_values(left, unit)
    vel_r, pres_r, enth_r, q_r = side_values(right, unit)
    root_l = jnp.sqrt(left[0])
    root_r = jnp.sqrt(right[0])
    per_sum = 1.0 / (root_l + root_r)
    a = root_l * per_sum
    b = root_r * per_sum
    vel = [a * x + b * y for x, y in zip(vel_l, vel_r)]
    enth = a * enth_l + b * enth_r
    dens = root_l * root_r
    q = dot3(vel, unit)
    kinetic = 0.5 * dot3(vel, vel)
    c_sq = GAMMA_LESS * (enth - kinetic)
    c = jnp.sqrt(c_sq)
    per_c_sq = 1.0 / c_sq
    d_pres = pres_r - pres_l
    d_dens = right[0] - left[0]
    d_vel = [y - x for x, y in zip(vel_l, vel_r)]
    d_q = dot3(d_vel, unit)
    fix = 0.01 * c_sq
    rel = q - grid
    slow = rel - c
    fast = rel + c
    wave_slow = jnp.sqrt(slow * slow + fix)
    wave_mid = jnp.sqrt(rel * rel + fix)
    wave_fast = jnp.sqrt(fast * fast + fix)
    half = 0.5 * per_c_sq
    cross = dens * c * d_q
    part_slow = wave_slow * ((d_pres - cross) * half)
    part_fast = wave_fast * ((d_pres + cross) * half)
    part_mid = wave_mid * (d_dens - d_pres * per_c_sq)
    shear = wave_mid * dens
    both = part_slow + part_fast
    total = both + part_mid
    diff = c * (part_fast - part_slow)
    move_l = q_l - grid
    move_r = q_r - grid
    along = pres_l + pres_r - diff + shear * d_q
    out = [left[0] * move_l + right[0] * move_r - total]
    for i in range(3):
        out.append(
            left[i + 1] * move_l
            + right[i + 1] * move_r
            + along * unit[i]
            - total * vel[i]
            - shear * d_vel[i]
        )
    out.append(
        left[4] * move_l
        + right[4] * move_r
        + pres_l * q_l
        + pres_r * q_r
        - both * enth
        - diff * q
        - part_mid * kinetic
        - shear * (dot3(vel, d_vel) - q * d_q)
    )
    scale = 0.5 * area
    return [scale * x for x in out]


def scatter(terms, where_cells, masked, total):
    lanes = where_cells & 127
    chunk = where_cells >> 7
    for v, x in enumerate(terms):
        upper = x.astype(BF16).astype(F32)
        for piece, part in enumerate((upper, x - upper)):
            for h in range(4):
                masked[pl.ds(h * 12 + piece * 6 + v, 8, stride=RS), :] = jnp.where(chunk == h, part, 0.0)
    slot = lax.broadcasted_iota(jnp.int32, (128, 128), 0)
    result = None
    for s in range(0, 8, 2):
        pair = (s, s + 1)
        left = jnp.concatenate([masked[i * RS : i * RS + 48, :].astype(BF16) for i in pair], axis=1)
        right = jnp.concatenate(
            [jnp.where(lanes[i : i + 1, :] == slot, 1.0, 0.0).astype(BF16) for i in pair], axis=1
        )
        part = lax.dot_general(left, right, (((1,), (1,)), ((), ())), preferred_element_type=F32)
        result = part if result is None else result + part
    total[...] += result


def kernel(
    remote,
    state,
    grad,
    adjacency,
    node_vel,
    face_normal,
    face_nodes,
    inner_cells,
    iface_cells,
    total,
    table,
    nodes,
    own,
    theirs,
    sweeps,
    halo,
    masked,
    send_sem,
    recv_sem,
    halo_send,
    halo_recv,
):
    if remote:
        zone = lax.axis_index("zone")
        dom = lax.axis_index("dom")
        n_dom = lax.axis_size("dom")
        nxt = lax.rem(dom + 1, n_dom)
        prv = lax.rem(dom + n_dom - 1, n_dom)

        def flip(at, bit):
            return at + bit * (1 - 2 * ((at // bit) % 2))

        peers = [
            (zone, flip(dom, 1)),
            (zone, flip(dom, 2)),
            (zone, flip(dom, 4)),
            (zone, flip(dom, 8)),
            (flip(zone, 1), dom),
            (zone, flip(dom, 16)),
        ]
        barrier = pltpu.get_barrier_semaphore()
        for peer in peers + [(zone, nxt), (zone, prv)]:
            pl.semaphore_signal(barrier, inc=1, device_id=peer, device_id_type=pl.DeviceIdType.MESH)

    def exchange(index):
        if remote:
            return pltpu.make_async_remote_copy(
                src_ref=own.at[index],
                dst_ref=theirs.at[index],
                send_sem=send_sem.at[index],
                recv_sem=recv_sem.at[index],
                device_id=peers[index],
                device_id_type=pl.DeviceIdType.MESH,
            )
        return pltpu.make_async_copy(own.at[index], theirs.at[index], recv_sem.at[index])

    def halo_copy(side):
        source = node_vel.at[:, 3 * (1 - side), :]
        if remote:
            return pltpu.make_async_remote_copy(
                src_ref=source,
                dst_ref=halo.at[side],
                send_sem=halo_send.at[side],
                recv_sem=halo_recv.at[side],
                device_id=(zone, prv if side else nxt),
                device_id_type=pl.DeviceIdType.MESH,
            )
        return pltpu.make_async_copy(source, halo.at[side], halo_recv.at[side])

    for v in range(5):
        for h in range(4):
            table[4 * v + h] = jnp.broadcast_to(state[v, h : h + 1, :], (8, CB))
    for b in range(NB):
        sums = None
        for k in range(K):
            near = jnp.full((5, CB), adjacency[k, 0, b], jnp.int32)
            block = state[:, 0, :]
            for other in range(1, NB):
                block = jnp.where(near == other, state[:, other, :], block)
            part = jnp.dot(block.astype(BF16), grad[b, k], preferred_element_type=F32)
            sums = part if sums is None else sums + part
        for v in range(5):
            for d in range(3):
                table[20 + 4 * (3 * v + d) + b] = jnp.broadcast_to(
                    sums[v : v + 1, d * CB : (d + 1) * CB], (8, CB)
                )

    def normal_of(tile):
        return [face_normal[d, rows8(tile), :] for d in range(3)]

    def cells_of(index, t):
        return iface_cells[index, rows8(t), :]

    if remote:
        pl.semaphore_wait(barrier, len(peers) + 2)
    for side in range(2):
        halo_copy(side).start()

    for index in SEND_ORDER:

        def own_tile(t, _, index=index):
            where = split_cells(cells_of(index, t))
            out = rebuild(table, where, normal_of(1 + RT * index + t))
            for v in range(5):
                own[index, v, rows8(t), :] = out[v]
            return 0

        lax.fori_loop(0, RT, own_tile, 0, unroll=RT)
        exchange(index).start()

    for d in range(3):
        for h in range(4):
            nodes[6 * d + 1 + h] = jnp.broadcast_to(node_vel[d, h : h + 1, :], (8, CB))
    for side in range(2):
        halo_copy(side).wait()
        if remote:
            inside = (dom != n_dom - 1) if side else (dom != 0)
        for d in range(3):
            row = jnp.broadcast_to(halo[side, d : d + 1, :], (8, CB))
            if remote:
                row = jnp.where(inside, row, 0.0)
            nodes[6 * d + 5 * side] = row

    def sweep_tile(tile, _):
        normal = normal_of(tile)
        sums = [None] * 3
        for corner in range(4):
            at = face_nodes[pl.ds(tile * 32 + corner, 8, stride=4), :]
            lanes = at & 127
            chunk = at >> 7
            for d in range(3):
                value = take(nodes[6 * d], lanes)
                for h in range(1, 6):
                    value = jnp.where(chunk == h, take(nodes[6 * d + h], lanes), value)
                sums[d] = value if corner == 0 else sums[d] + value
        sweeps[rows8(tile), :] = (0.25 * STEP_SIZE) * dot3(normal, sums)
        return 0

    lax.fori_loop(0, TILES, sweep_tile, 0, unroll=5)

    total[...] = jnp.zeros_like(total)

    normal = normal_of(0)
    sweep = sweeps[0:8, :]
    left_cells = inner_cells[pl.ds(0, 8, stride=2), :]
    right_cells = inner_cells[pl.ds(1, 8, stride=2), :]
    left = rebuild(table, split_cells(left_cells), normal)
    right = rebuild(table, split_cells(right_cells), [-x for x in normal])
    flux = roe_flux(left, right, normal, sweep)
    scatter([-x for x in flux] + [sweep], left_cells, masked.at[0], total)
    scatter(flux + [-sweep], right_cells, masked.at[1], total)

    for index in FLUX_ORDER:
        exchange(index).wait()

        def flux_tile(t, half, index=index):
            tile = 1 + RT * index + t
            ours = [own[index, v, rows8(t), :] for v in range(5)]
            other = [theirs[index, v, rows8(t), :] for v in range(5)]
            sweep = sweeps[rows8(tile), :]
            flux = roe_flux(ours, other, normal_of(tile), sweep)
            scatter([-x for x in flux] + [sweep], cells_of(index, t), masked.at[half], total)

        def flux_pair(t, _):
            flux_tile(2 * t, 0)
            flux_tile(2 * t + 1, 1)
            return 0

        lax.fori_loop(0, RT // 2, flux_pair, 0)


def finish(total, state, volume, counts, content, new_volume):
    live = counts[0, 0]
    for h in range(4):
        on = jnp.full((8, CB), h, jnp.int32) < live
        sums = total[h * 12 : h * 12 + 6, :] + total[h * 12 + 6 : h * 12 + 12, :]
        room = volume[h : h + 1, :]
        content[:, h, :] = room * state[:, h, :] + jnp.where(on[0:5], STEP_SIZE * sums[0:5, :], 0.0)
        new_volume[h : h + 1, :] = room + jnp.where(on[0:1], sums[5:6, :], 0.0)


def section(remote, state, grad, adjacency, node_vel, face_normal, face_nodes, inner_cells, iface_cells, volume, counts):
    vmem = pl.BlockSpec(memory_space=pltpu.VMEM)
    smem = pl.BlockSpec(memory_space=pltpu.SMEM)
    params = dict(vmem_limit_bytes=60 << 20)
    if remote:
        params.update(collective_id=0, has_side_effects=True)
    total = pl.pallas_call(
        functools.partial(kernel, remote),
        out_shape=jax.ShapeDtypeStruct((48, CB), F32),
        in_specs=[vmem, vmem, smem, vmem, vmem, vmem, vmem, vmem],
        out_specs=vmem,
        scratch_shapes=[
            pltpu.VMEM((80, 8, CB), F32),
            pltpu.VMEM((18, 8, CB), F32),
            pltpu.VMEM((ROUNDS, 5, RT * 8, CB), F32),
            pltpu.VMEM((ROUNDS, 5, RT * 8, CB), F32),
            pltpu.VMEM((TILES * 8, CB), F32),
            pltpu.VMEM((2, 3, HN), F32),
            pltpu.VMEM((2, 8 * RS, CB), F32),
            pltpu.SemaphoreType.DMA((ROUNDS,)),
            pltpu.SemaphoreType.DMA((ROUNDS,)),
            pltpu.SemaphoreType.DMA((2,)),
            pltpu.SemaphoreType.DMA((2,)),
        ],
        compiler_params=pltpu.CompilerParams(**params),
    )(state, grad, adjacency, node_vel, face_normal, face_nodes, inner_cells, iface_cells)
    return pl.pallas_call(
        finish,
        out_shape=(
            jax.ShapeDtypeStruct((5, NB, CB), F32),
            jax.ShapeDtypeStruct((NB, CB), F32),
        ),
        in_specs=[vmem, vmem, vmem, smem],
        out_specs=(vmem, vmem),
    )(total, state, volume, counts)


def by_chunk(rows):
    count, length = rows.shape
    return rows.reshape(count, length // CB, CB).swapaxes(0, 1).reshape(count * length // CB, CB)


def shards(
    state,
    grad_op,
    adjacency,
    node_vel,
    face_normal,
    face_nodes,
    inner_cells,
    iface_cells,
    cell_volume,
    block_counts,
):
    content, new_volume = section(
        True,
        state.reshape(5, NB, CB),
        grad_op.reshape(NB, K, CB, 3 * CB),
        jnp.swapaxes(adjacency, 2, 3).reshape(K, 1, NB),
        node_vel.reshape(3, NB, CB),
        face_normal.reshape(3, TILES * 8, CB),
        by_chunk(face_nodes[0, 0]),
        by_chunk(inner_cells[0, 0]),
        iface_cells.reshape(ROUNDS, RT * 8, CB),
        cell_volume.reshape(NB, CB),
        block_counts,
    )
    return (content.reshape(1, 1, 5, NN), new_volume.reshape(1, 1, NN))


def solution(mesh):
    return jax.shard_map(
        shards,
        mesh=mesh,
        in_specs=(
            P("zone", "dom", None, None),
            P("zone", "dom", None, None, None, None),
            P("zone", "dom", None, None),
            P("zone", "dom", None, None),
            P("zone", "dom", None, None),
            P("zone", "dom", None, None),
            P("zone", "dom", None, None),
            P("zone", "dom", None, None),
            P("zone", "dom", None),
            P("zone", "dom"),
        ),
        out_specs=(P("zone", "dom", None, None), P("zone", "dom", None)),
        check_vma=False,
    )
```

```python
import functools

import jax
import jax.numpy as jnp
from jax import lax
from jax.experimental import pallas as pl
from jax.experimental.pallas import tpu as pltpu
from jax.sharding import PartitionSpec as P

CB = 128
NB = 4
K = 3
ROUNDS = 6
HN = 128
NN = 512
RT = 4
TILES = 25
RS = 56

STEP_SIZE = 0.25
RECON_GAIN = 0.2
GAMMA_LESS = 0.4

SEND_ORDER = (2, 4, 1, 5, 3, 0)
FLUX_ORDER = (0, 3, 5, 4, 1, 2)

F32 = jnp.float32
BF16 = jnp.bfloat16


def take(row, lanes):
    return jnp.take_along_axis(row, lanes, axis=1, mode="promise_in_bounds")


def rows8(tile):
    return pl.ds(pl.multiple_of(tile * 8, 8), 8)


def split_cells(cells):
    return cells & 127, (cells & 128) != 0, (cells & 256) != 0


def pick(table, first, where):
    lanes, odd, upper = where
    low = jnp.where(odd, take(table[first + 1], lanes), take(table[first], lanes))
    high = jnp.where(odd, take(table[first + 3], lanes), take(table[first + 2], lanes))
    return jnp.where(upper, high, low)


def rebuild(table, where, normal):
    cons = [pick(table, 4 * v, where) for v in range(5)]
    delta = []
    for v in range(5):
        parts = [pick(table, 20 + 4 * (3 * v + d), where) * normal[d] for d in range(3)]
        delta.append(parts[0] + parts[1] + parts[2])
    per_dens = 1.0 / cons[0]
    gain = RECON_GAIN * cons[0]
    out = [cons[0] + gain * jnp.tanh(delta[0] * per_dens)]
    for v in range(1, 4):
        out.append(cons[v] + gain * jnp.tanh(delta[v] * per_dens))
    out.append(cons[4] + RECON_GAIN * cons[4] * jnp.tanh(delta[4] / cons[4]))
    return out


def dot3(a, b):
    return a[0] * b[0] + a[1] * b[1] + a[2] * b[2]


def side_values(cons, unit):
    per_dens = 1.0 / cons[0]
    vel = [cons[i] * per_dens for i in (1, 2, 3)]
    pres = GAMMA_LESS * (cons[4] - 0.5 * dot3(cons[1:4], vel))
    enth = (cons[4] + pres) * per_dens
    return vel, pres, enth, dot3(vel, unit)


def roe_flux(left, right, normal, sweep):
    area_sq = dot3(normal, normal)
    per_area = lax.rsqrt(area_sq)
    area = area_sq * per_area
    unit = [x * per_area for x in normal]
    grid = sweep * per_area * (1.0 / STEP_SIZE)
    vel_l, pres_l, enth_l, q_l = side_values(left, unit)
    vel_r, pres_r, enth_r, q_r = side_values(right, unit)
    root_l = jnp.sqrt(left[0])
    root_r = jnp.sqrt(right[0])
    per_sum = 1.0 / (root_l + root_r)
    a = root_l * per_sum
    b = root_r * per_sum
    vel = [a * x + b * y for x, y in zip(vel_l, vel_r)]
    enth = a * enth_l + b * enth_r
    dens = root_l * root_r
    q = dot3(vel, unit)
    kinetic = 0.5 * dot3(vel, vel)
    c_sq = GAMMA_LESS * (enth - kinetic)
    c = jnp.sqrt(c_sq)
    per_c_sq = 1.0 / c_sq
    d_pres = pres_r - pres_l
    d_dens = right[0] - left[0]
    d_vel = [y - x for x, y in zip(vel_l, vel_r)]
    d_q = dot3(d_vel, unit)
    fix = 0.01 * c_sq
    rel = q - grid
    slow = rel - c
    fast = rel + c
    wave_slow = jnp.sqrt(slow * slow + fix)
    wave_mid = jnp.sqrt(rel * rel + fix)
    wave_fast = jnp.sqrt(fast * fast + fix)
    half = 0.5 * per_c_sq
    cross = dens * c * d_q
    part_slow = wave_slow * ((d_pres - cross) * half)
    part_fast = wave_fast * ((d_pres + cross) * half)
    part_mid = wave_mid * (d_dens - d_pres * per_c_sq)
    shear = wave_mid * dens
    both = part_slow + part_fast
    total = both + part_mid
    diff = c * (part_fast - part_slow)
    move_l = q_l - grid
    move_r = q_r - grid
    along = pres_l + pres_r - diff + shear * d_q
    out = [left[0] * move_l + right[0] * move_r - total]
    for i in range(3):
        out.append(
            left[i + 1] * move_l
            + right[i + 1] * move_r
            + along * unit[i]
            - total * vel[i]
            - shear * d_vel[i]
        )
    out.append(
        left[4] * move_l
        + right[4] * move_r
        + pres_l * q_l
        + pres_r * q_r
        - both * enth
        - diff * q
        - part_mid * kinetic
        - shear * (dot3(vel, d_vel) - q * d_q)
    )
    scale = 0.5 * area
    return [scale * x for x in out]


def scatter(terms, where_cells, masked, total):
    lanes = where_cells & 127
    chunk = where_cells >> 7
    for v, x in enumerate(terms):
        upper = x.astype(BF16).astype(F32)
        for piece, part in enumerate((upper, x - upper)):
            for h in range(4):
                masked[pl.ds(h * 12 + piece * 6 + v, 8, stride=RS), :] = jnp.where(chunk == h, part, 0.0)
    slot = lax.broadcasted_iota(jnp.int32, (128, 128), 0)
    result = None
    for s in range(0, 8, 2):
        pair = (s, s + 1)
        left = jnp.concatenate([masked[i * RS : i * RS + 48, :].astype(BF16) for i in pair], axis=1)
        right = jnp.concatenate(
            [jnp.where(lanes[i : i + 1, :] == slot, 1.0, 0.0).astype(BF16) for i in pair], axis=1
        )
        part = lax.dot_general(left, right, (((1,), (1,)), ((), ())), preferred_element_type=F32)
        result = part if result is None else result + part
    total[...] += result


def kernel(
    remote,
    state_hbm,
    grad_hbm,
    adjacency_hbm,
    node_vel_hbm,
    face_normal_hbm,
    face_nodes_hbm,
    inner_cells_hbm,
    iface_cells_hbm,
    total,
    state,
    grad,
    adjacency,
    node_vel,
    face_normal,
    face_nodes,
    inner_cells,
    iface_cells,
    table,
    nodes,
    own,
    theirs,
    sweeps,
    halo,
    masked,
    send_sem,
    recv_sem,
    halo_send,
    halo_recv,
    stage_sem,
    grad_sem,
):
    def stage(source, target, sem):
        copy = pltpu.make_async_copy(source, target, sem)
        copy.start()
        return copy

    staged_state = stage(state_hbm, state, stage_sem.at[0])
    staged_adjacency = stage(adjacency_hbm, adjacency, stage_sem.at[1])
    staged_grad = [stage(grad_hbm.at[b], grad.at[b], grad_sem.at[b]) for b in range(NB)]
    staged_cells = stage(iface_cells_hbm, iface_cells, stage_sem.at[2])
    staged_normal = stage(face_normal_hbm, face_normal, stage_sem.at[3])
    staged_vel = stage(node_vel_hbm, node_vel, stage_sem.at[4])
    staged_pairs = stage(inner_cells_hbm, inner_cells, stage_sem.at[5])
    staged_nodes = stage(face_nodes_hbm, face_nodes, stage_sem.at[6])

    if remote:
        zone = lax.axis_index("zone")
        dom = lax.axis_index("dom")
        n_dom = lax.axis_size("dom")
        nxt = lax.rem(dom + 1, n_dom)
        prv = lax.rem(dom + n_dom - 1, n_dom)

        def flip(at, bit):
            return at + bit * (1 - 2 * ((at // bit) % 2))

        peers = [
            (zone, flip(dom, 1)),
            (zone, flip(dom, 2)),
            (zone, flip(dom, 4)),
            (zone, flip(dom, 8)),
            (flip(zone, 1), dom),
            (zone, flip(dom, 16)),
        ]
        barrier = pltpu.get_barrier_semaphore()
        for peer in peers + [(zone, nxt), (zone, prv)]:
            pl.semaphore_signal(barrier, inc=1, device_id=peer, device_id_type=pl.DeviceIdType.MESH)

    def exchange(index):
        if remote:
            return pltpu.make_async_remote_copy(
                src_ref=own.at[index],
                dst_ref=theirs.at[index],
                send_sem=send_sem.at[index],
                recv_sem=recv_sem.at[index],
                device_id=peers[index],
                device_id_type=pl.DeviceIdType.MESH,
            )
        return pltpu.make_async_copy(own.at[index], theirs.at[index], recv_sem.at[index])

    def halo_copy(side):
        source = node_vel.at[:, 3 * (1 - side), :]
        if remote:
            return pltpu.make_async_remote_copy(
                src_ref=source,
                dst_ref=halo.at[side],
                send_sem=halo_send.at[side],
                recv_sem=halo_recv.at[side],
                device_id=(zone, prv if side else nxt),
                device_id_type=pl.DeviceIdType.MESH,
            )
        return pltpu.make_async_copy(source, halo.at[side], halo_recv.at[side])

    staged_state.wait()
    staged_adjacency.wait()
    for v in range(5):
        for h in range(4):
            table[4 * v + h] = jnp.broadcast_to(state[v, h : h + 1, :], (8, CB))
    for b in range(NB):
        sums = None
        staged_grad[b].wait()
        for k in range(K):
            near = jnp.broadcast_to(adjacency[k, :, b : b + 1], (5, CB))
            block = state[:, 0, :]
            for other in range(1, NB):
                block = jnp.where(near == other, state[:, other, :], block)
            part = jnp.dot(block.astype(BF16), grad[b, k], preferred_element_type=F32)
            sums = part if sums is None else sums + part
        for v in range(5):
            for d in range(3):
                table[20 + 4 * (3 * v + d) + b] = jnp.broadcast_to(
                    sums[v : v + 1, d * CB : (d + 1) * CB], (8, CB)
                )

    def normal_of(tile):
        return [face_normal[d, rows8(tile), :] for d in range(3)]

    def cells_of(index, t):
        return iface_cells[index, rows8(t), :]

    if remote:
        pl.semaphore_wait(barrier, len(peers) + 2)
    staged_vel.wait()
    for side in range(2):
        halo_copy(side).start()

    staged_cells.wait()
    staged_normal.wait()

    for index in SEND_ORDER:

        def own_tile(t, _, index=index):
            where = split_cells(cells_of(index, t))
            out = rebuild(table, where, normal_of(1 + RT * index + t))
            for v in range(5):
                own[index, v, rows8(t), :] = out[v]
            return 0

        lax.fori_loop(0, RT, own_tile, 0, unroll=RT)
        exchange(index).start()

    for d in range(3):
        for h in range(4):
            nodes[6 * d + 1 + h] = jnp.broadcast_to(node_vel[d, h : h + 1, :], (8, CB))
    for side in range(2):
        halo_copy(side).wait()
        if remote:
            inside = (dom != n_dom - 1) if side else (dom != 0)
        for d in range(3):
            row = jnp.broadcast_to(halo[side, d : d + 1, :], (8, CB))
            if remote:
                row = jnp.where(inside, row, 0.0)
            nodes[6 * d + 5 * side] = row

    staged_nodes.wait()
    staged_pairs.wait()

    def sweep_tile(tile, _):
        normal = normal_of(tile)
        sums = [None] * 3
        for corner in range(4):
            at = face_nodes[pl.ds(tile * 32 + corner, 8, stride=4), :]
            lanes = at & 127
            chunk = at >> 7
            for d in range(3):
                value = take(nodes[6 * d], lanes)
                for h in range(1, 6):
                    value = jnp.where(chunk == h, take(nodes[6 * d + h], lanes), value)
                sums[d] = value if corner == 0 else sums[d] + value
        sweeps[rows8(tile), :] = (0.25 * STEP_SIZE) * dot3(normal, sums)
        return 0

    def first_sweeps(t, _):
        sweep_tile(1 + RT * FLUX_ORDER[0] + t, 0)
        return 0

    sweep_tile(0, 0)
    lax.fori_loop(0, RT, first_sweeps, 0, unroll=RT)

    total[...] = jnp.zeros_like(total)

    normal = normal_of(0)
    sweep = sweeps[0:8, :]
    left_cells = inner_cells[pl.ds(0, 8, stride=2), :]
    right_cells = inner_cells[pl.ds(1, 8, stride=2), :]
    left = rebuild(table, split_cells(left_cells), normal)
    right = rebuild(table, split_cells(right_cells), [-x for x in normal])
    flux = roe_flux(left, right, normal, sweep)
    scatter([-x for x in flux] + [sweep], left_cells, masked.at[0], total)
    scatter(flux + [-sweep], right_cells, masked.at[1], total)

    for place, index in enumerate(FLUX_ORDER):
        later = FLUX_ORDER[place + 1] if place + 1 < ROUNDS else None
        exchange(index).wait()

        def flux_tile(t, half, index=index):
            tile = 1 + RT * index + t
            ours = [own[index, v, rows8(t), :] for v in range(5)]
            other = [theirs[index, v, rows8(t), :] for v in range(5)]
            sweep = sweeps[rows8(tile), :]
            flux = roe_flux(ours, other, normal_of(tile), sweep)
            scatter([-x for x in flux] + [sweep], cells_of(index, t), masked.at[half], total)

        def flux_pair(t, _, later=later):
            if later is not None:
                for i in range(2):
                    sweep_tile(1 + RT * later + 2 * t + i, 0)
            flux_tile(2 * t, 0)
            flux_tile(2 * t + 1, 1)
            return 0

        lax.fori_loop(0, RT // 2, flux_pair, 0)


def finish(total, state, volume, counts, content, new_volume):
    live = jnp.broadcast_to(counts[...], (8, CB))
    for h in range(4):
        on = live > h
        sums = total[h * 12 : h * 12 + 6, :] + total[h * 12 + 6 : h * 12 + 12, :]
        room = volume[h : h + 1, :]
        content[:, h, :] = room * state[:, h, :] + jnp.where(on[0:5], STEP_SIZE * sums[0:5, :], 0.0)
        new_volume[h : h + 1, :] = room + jnp.where(on[0:1], sums[5:6, :], 0.0)


def section(remote, state, grad, adjacency, node_vel, face_normal, face_nodes, inner_cells, iface_cells, volume, counts):
    vmem = pl.BlockSpec(memory_space=pltpu.VMEM)
    hbm = pl.BlockSpec(memory_space=pltpu.HBM)
    params = dict(vmem_limit_bytes=60 << 20)
    if remote:
        params.update(collective_id=0, has_side_effects=True)
    inputs = (state, grad, adjacency, node_vel, face_normal, face_nodes, inner_cells, iface_cells)
    total = pl.pallas_call(
        functools.partial(kernel, remote),
        out_shape=jax.ShapeDtypeStruct((48, CB), F32),
        in_specs=[hbm] * 8,
        out_specs=vmem,
        scratch_shapes=[
            *(pltpu.VMEM(x.shape, x.dtype) for x in inputs),
            pltpu.VMEM((80, 8, CB), F32),
            pltpu.VMEM((18, 8, CB), F32),
            pltpu.VMEM((ROUNDS, 5, RT * 8, CB), F32),
            pltpu.VMEM((ROUNDS, 5, RT * 8, CB), F32),
            pltpu.VMEM((TILES * 8, CB), F32),
            pltpu.VMEM((2, 3, HN), F32),
            pltpu.VMEM((2, 8 * RS, CB), F32),
            pltpu.SemaphoreType.DMA((ROUNDS,)),
            pltpu.SemaphoreType.DMA((ROUNDS,)),
            pltpu.SemaphoreType.DMA((2,)),
            pltpu.SemaphoreType.DMA((2,)),
            pltpu.SemaphoreType.DMA((7,)),
            pltpu.SemaphoreType.DMA((NB,)),
        ],
        compiler_params=pltpu.CompilerParams(**params),
    )(*inputs)
    return pl.pallas_call(
        finish,
        out_shape=(
            jax.ShapeDtypeStruct((5, NB, CB), F32),
            jax.ShapeDtypeStruct((NB, CB), F32),
        ),
        in_specs=[vmem] * 4,
        out_specs=(vmem, vmem),
    )(total, state, volume, counts)


def by_chunk(rows):
    count, length = rows.shape
    return rows.reshape(count, length // CB, CB).swapaxes(0, 1).reshape(count * length // CB, CB)


def shards(
    state,
    grad_op,
    adjacency,
    node_vel,
    face_normal,
    face_nodes,
    inner_cells,
    iface_cells,
    cell_volume,
    block_counts,
):
    content, new_volume = section(
        True,
        state.reshape(5, NB, CB),
        grad_op.reshape(NB, K, CB, 3 * CB),
        jnp.swapaxes(adjacency, 2, 3).reshape(K, 1, NB),
        node_vel.reshape(3, NB, CB),
        face_normal.reshape(3, TILES * 8, CB),
        by_chunk(face_nodes[0, 0]),
        by_chunk(inner_cells[0, 0]),
        iface_cells.reshape(ROUNDS, RT * 8, CB),
        cell_volume.reshape(NB, CB),
        block_counts,
    )
    return (content.reshape(1, 1, 5, NN), new_volume.reshape(1, 1, NN))


def solution(mesh):
    return jax.shard_map(
        shards,
        mesh=mesh,
        in_specs=(
            P("zone", "dom", None, None),
            P("zone", "dom", None, None, None, None),
            P("zone", "dom", None, None),
            P("zone", "dom", None, None),
            P("zone", "dom", None, None),
            P("zone", "dom", None, None),
            P("zone", "dom", None, None),
            P("zone", "dom", None, None),
            P("zone", "dom", None),
            P("zone", "dom"),
        ),
        out_specs=(P("zone", "dom", None, None), P("zone", "dom", None)),
        check_vma=False,
    )
```

```python
import functools

import jax
import jax.numpy as jnp
from jax import lax
from jax.experimental import pallas as pl
from jax.experimental.pallas import tpu as pltpu
from jax.sharding import PartitionSpec as P

CB = 128
NB = 4
K = 3
ROUNDS = 6
HN = 128
NN = 512
RT = 4
TILES = 25
RS = 24

STEP_SIZE = 0.25
RECON_GAIN = 0.2
GAMMA_LESS = 0.4

SEND_ORDER = (2, 4, 1, 5, 3, 0)
FLUX_ORDER = (0, 3, 5, 4, 1, 2)

REST_AFTER = 1
LATE_HOLDS = (4, 1)
CROSSING = 2
VMEM_LIMIT = 60 << 20

F32 = jnp.float32
BF16 = jnp.bfloat16


def take(row, lanes):
    return jnp.take_along_axis(row, lanes, axis=1, mode="promise_in_bounds")


def rows8(tile):
    return pl.ds(pl.multiple_of(tile * 8, 8), 8)


def split_cells(cells):
    return cells & 127, (cells & 128) != 0, (cells & 256) != 0


def pick(table, first, where):
    lanes, odd, upper = where
    low = jnp.where(odd, take(table[first + 1], lanes), take(table[first], lanes))
    high = jnp.where(odd, take(table[first + 3], lanes), take(table[first + 2], lanes))
    return jnp.where(upper, high, low)


def rebuild(table, where, normal):
    cons = [pick(table, 4 * v, where) for v in range(5)]
    delta = []
    for v in range(5):
        parts = [pick(table, 20 + 4 * (3 * v + d), where) * normal[d] for d in range(3)]
        delta.append(parts[0] + parts[1] + parts[2])
    per_dens = 1.0 / cons[0]
    gain = RECON_GAIN * cons[0]
    out = [cons[0] + gain * jnp.tanh(delta[0] * per_dens)]
    for v in range(1, 4):
        out.append(cons[v] + gain * jnp.tanh(delta[v] * per_dens))
    out.append(cons[4] + RECON_GAIN * cons[4] * jnp.tanh(delta[4] / cons[4]))
    return out


def dot3(a, b):
    return a[0] * b[0] + a[1] * b[1] + a[2] * b[2]


def side_values(cons, unit):
    per_dens = 1.0 / cons[0]
    vel = [cons[i] * per_dens for i in (1, 2, 3)]
    pres = GAMMA_LESS * (cons[4] - 0.5 * dot3(cons[1:4], vel))
    enth = (cons[4] + pres) * per_dens
    return vel, pres, enth, dot3(vel, unit)


def roe_flux(left, right, normal, sweep):
    area_sq = dot3(normal, normal)
    per_area = lax.rsqrt(area_sq)
    area = area_sq * per_area
    unit = [x * per_area for x in normal]
    grid = sweep * per_area * (1.0 / STEP_SIZE)
    vel_l, pres_l, enth_l, q_l = side_values(left, unit)
    vel_r, pres_r, enth_r, q_r = side_values(right, unit)
    root_l = jnp.sqrt(left[0])
    root_r = jnp.sqrt(right[0])
    per_sum = 1.0 / (root_l + root_r)
    a = root_l * per_sum
    b = root_r * per_sum
    vel = [a * x + b * y for x, y in zip(vel_l, vel_r)]
    enth = a * enth_l + b * enth_r
    dens = root_l * root_r
    q = dot3(vel, unit)
    kinetic = 0.5 * dot3(vel, vel)
    c_sq = GAMMA_LESS * (enth - kinetic)
    c = jnp.sqrt(c_sq)
    per_c_sq = 1.0 / c_sq
    d_pres = pres_r - pres_l
    d_dens = right[0] - left[0]
    d_vel = [y - x for x, y in zip(vel_l, vel_r)]
    d_q = dot3(d_vel, unit)
    fix = 0.01 * c_sq
    rel = q - grid
    slow = rel - c
    fast = rel + c
    wave_slow = jnp.sqrt(slow * slow + fix)
    wave_mid = jnp.sqrt(rel * rel + fix)
    wave_fast = jnp.sqrt(fast * fast + fix)
    half = 0.5 * per_c_sq
    cross = dens * c * d_q
    part_slow = wave_slow * ((d_pres - cross) * half)
    part_fast = wave_fast * ((d_pres + cross) * half)
    part_mid = wave_mid * (d_dens - d_pres * per_c_sq)
    shear = wave_mid * dens
    both = part_slow + part_fast
    total = both + part_mid
    diff = c * (part_fast - part_slow)
    move_l = q_l - grid
    move_r = q_r - grid
    along = pres_l + pres_r - diff + shear * d_q
    out = [left[0] * move_l + right[0] * move_r - total]
    for i in range(3):
        out.append(
            left[i + 1] * move_l
            + right[i + 1] * move_r
            + along * unit[i]
            - total * vel[i]
            - shear * d_vel[i]
        )
    out.append(
        left[4] * move_l
        + right[4] * move_r
        + pres_l * q_l
        + pres_r * q_r
        - both * enth
        - diff * q
        - part_mid * kinetic
        - shear * (dot3(vel, d_vel) - q * d_q)
    )
    scale = 0.5 * area
    return [scale * x for x in out]


def scatter(terms, where_cells, split, total):
    for v, x in enumerate(terms):
        upper = x.astype(BF16).astype(F32)
        split[pl.ds(v, 8, stride=RS), :] = upper
        split[pl.ds(v + 6, 8, stride=RS), :] = x - upper
    lanes = (where_cells & 127).astype(F32)
    chunk = (where_cells >> 7).astype(F32)
    slot = lax.broadcasted_iota(jnp.int32, (CB, CB), 0).astype(F32).astype(BF16)
    one, zero = jnp.ones((), BF16), jnp.zeros((), BF16)
    result = None
    for s in range(0, 8, 2):
        left, right = [], []
        for i in (s, s + 1):
            rows = split[i * RS : i * RS + 16, :].astype(BF16)
            home = jnp.broadcast_to(chunk[i : i + 1, :], (16, CB)).astype(BF16)
            left.append(jnp.concatenate([jnp.where(home == h, rows, zero) for h in range(4)], axis=0))
            at = jnp.broadcast_to(lanes[i : i + 1, :], (CB, CB)).astype(BF16)
            right.append(jnp.where(at == slot, one, zero))
        left, right = jnp.concatenate(left, axis=1), jnp.concatenate(right, axis=1)
        part = lax.dot_general(left, right, (((1,), (1,)), ((), ())), preferred_element_type=F32)
        result = part if result is None else result + part
    total[...] += result


def kernel(
    remote,
    state_hbm,
    grad_hbm,
    adjacency_hbm,
    node_vel_hbm,
    face_normal_hbm,
    face_nodes_hbm,
    inner_cells_hbm,
    iface_cells_hbm,
    total,
    state,
    grad,
    adjacency,
    node_vel,
    face_normal,
    face_nodes,
    inner_cells,
    iface_cells,
    table,
    nodes,
    own,
    theirs,
    sweeps,
    halo,
    split,
    send_sem,
    recv_sem,
    halo_send,
    halo_recv,
    stage_sem,
    grad_sem,
    ready,
):
    def stage(source, target, sem):
        copy = pltpu.make_async_copy(source, target, sem)
        copy.start()
        return copy

    halo[...] = jnp.zeros_like(halo)
    first = SEND_ORDER[0]
    top, bottom = 8 * (1 + RT * first), 8 * (1 + RT * (first + 1))

    def piece(source, target, at, sem):
        return stage(source.at[at], target.at[at], sem)

    staged_state = stage(state_hbm, state, stage_sem.at[0])
    staged_adjacency = stage(adjacency_hbm, adjacency, stage_sem.at[1])
    staged_grad = [stage(grad_hbm.at[b], grad.at[b], grad_sem.at[b]) for b in range(NB)]
    staged_first = [
        piece(iface_cells_hbm, iface_cells, pl.ds(first, 1), stage_sem.at[2]),
        piece(face_normal_hbm, face_normal, (slice(None), pl.ds(top, bottom - top)), stage_sem.at[3]),
    ]

    def stage_rest():
        return [
            piece(iface_cells_hbm, iface_cells, pl.ds(first + 1, ROUNDS - first - 1), stage_sem.at[4]),
            piece(face_normal_hbm, face_normal, (slice(None), pl.ds(bottom, TILES * 8 - bottom)), stage_sem.at[5]),
            piece(iface_cells_hbm, iface_cells, pl.ds(0, first), stage_sem.at[6]),
            piece(face_normal_hbm, face_normal, (slice(None), pl.ds(0, top)), stage_sem.at[7]),
        ], [
            stage(node_vel_hbm, node_vel, stage_sem.at[8]),
            stage(inner_cells_hbm, inner_cells, stage_sem.at[9]),
            stage(face_nodes_hbm, face_nodes, stage_sem.at[10]),
        ]

    if remote:
        zone = lax.axis_index("zone")
        dom = lax.axis_index("dom")
        n_dom = lax.axis_size("dom")
        nxt = lax.rem(dom + 1, n_dom)
        prv = lax.rem(dom + n_dom - 1, n_dom)
        has_nxt = 1 - (dom + 1) // n_dom
        has_prv = 1 - (n_dom - dom) // n_dom

        def flip(at, bit):
            return at + bit * (1 - 2 * ((at // bit) % 2))

        peers = [
            (zone, flip(dom, 1)),
            (zone, flip(dom, 2)),
            (zone, flip(dom, 4)),
            (zone, flip(dom, 8)),
            (flip(zone, 1), dom),
            (zone, flip(dom, 16)),
        ]
        def is_late(at):
            return (at // 4) % 2

        late = is_late(dom)
        early = 1 - late
        late_nxt = is_late(nxt)
        late_prv = is_late(prv)

        def signal(sem, peer):
            pl.semaphore_signal(sem, inc=1, device_id=peer, device_id_type=pl.DeviceIdType.MESH)

        barrier = pltpu.get_barrier_semaphore()
        for index in (4, 1, 0, 3, 5):
            signal(barrier, peers[index])

        @pl.when(early == 1)
        def _():
            signal(barrier, peers[2])

        @pl.when(has_nxt * (early + late_nxt) > 0)
        def _():
            signal(barrier, (zone, nxt))

        @pl.when(has_prv * (early + late_prv) > 0)
        def _():
            signal(barrier, (zone, prv))

    def exchange(index, half=None):
        if half is None:
            at, sem = pl.ds(2 * index, 2), 2 * index
        else:
            at = sem = 2 * index + half
        if remote:
            return pltpu.make_async_remote_copy(
                src_ref=own.at[at],
                dst_ref=theirs.at[at],
                send_sem=send_sem.at[sem],
                recv_sem=recv_sem.at[sem],
                device_id=peers[index],
                device_id_type=pl.DeviceIdType.MESH,
            )
        return pltpu.make_async_copy(own.at[at], theirs.at[at], recv_sem.at[sem])

    def halo_copy(side):
        source = node_vel_hbm.at[:, 3 * (1 - side), :]
        if remote:
            return pltpu.make_async_remote_copy(
                src_ref=source,
                dst_ref=halo.at[side],
                send_sem=halo_send.at[side],
                recv_sem=halo_recv.at[side],
                device_id=(zone, prv if side else nxt),
                device_id_type=pl.DeviceIdType.MESH,
            )
        return pltpu.make_async_copy(source, halo.at[side], halo_recv.at[side])

    def enter():
        meet_nxt = has_nxt * (1 - early * late_nxt)
        meet_prv = has_prv * (1 - early * late_prv)
        pl.semaphore_wait(barrier, 5 + late + meet_nxt + meet_prv)

        @pl.when(late == 1)
        def _():
            signal(ready.at[0], peers[2])

        @pl.when(late * (1 - late_nxt) * has_nxt == 1)
        def _():
            signal(ready.at[1], (zone, nxt))

        @pl.when(late * (1 - late_prv) * has_prv == 1)
        def _():
            signal(ready.at[2], (zone, prv))

        @pl.when(meet_nxt == 1)
        def _():
            halo_copy(0).start()

        @pl.when(meet_prv == 1)
        def _():
            halo_copy(1).start()

    def cross(what):
        if what == 0:

            @pl.when(early * late_nxt * has_nxt == 1)
            def _():
                pl.semaphore_wait(ready.at[2], 1)
                halo_copy(0).start()

        elif what == 1:

            @pl.when(early * late_prv * has_prv == 1)
            def _():
                pl.semaphore_wait(ready.at[1], 1)
                halo_copy(1).start()

        else:

            @pl.when(early == 1)
            def _():
                pl.semaphore_wait(ready.at[0], 1)
                for half in range(2):
                    exchange(CROSSING, half).start()

    if remote:
        pl.when(late == 1)(enter)

    staged_state.wait()
    staged_adjacency.wait()
    for v in range(5):
        for h in range(4):
            table[4 * v + h] = jnp.broadcast_to(state[v, h : h + 1, :], (8, CB))
    for b in range(NB):
        sums = None
        staged_grad[b].wait()
        if b == REST_AFTER:
            staged_faces, staged_late = stage_rest()
        for k in range(K):
            near = jnp.broadcast_to(adjacency[k, :, b : b + 1], (5, CB))
            block = state[:, 0, :]
            for other in range(1, NB):
                block = jnp.where(near == other, state[:, other, :], block)
            part = jnp.dot(block.astype(BF16), grad[b, k], preferred_element_type=F32)
            sums = part if sums is None else sums + part
        for v in range(5):
            for d in range(3):
                table[20 + 4 * (3 * v + d) + b] = jnp.broadcast_to(
                    sums[v : v + 1, d * CB : (d + 1) * CB], (8, CB)
                )

    def normal_of(tile):
        return [face_normal[d, rows8(tile), :] for d in range(3)]

    def cells_of(index, t):
        return iface_cells[index, rows8(t), :]

    if remote:
        pl.when(early == 1)(enter)
    else:
        for side in range(2):
            halo_copy(side).start()

    for copy in staged_first:
        copy.wait()

    for index in SEND_ORDER:
        if index == SEND_ORDER[1]:
            for copy in staged_faces:
                copy.wait()

        for half in range(2):
            for t in range(2):
                tile = 2 * half + t
                where = split_cells(cells_of(index, tile))
                out = rebuild(table, where, normal_of(1 + RT * index + tile))
                for v in range(5):
                    own[2 * index + half, v, rows8(t), :] = out[v]
            if index == CROSSING:
                if remote:

                    @pl.when(late == 1)
                    def _(half=half):
                        exchange(CROSSING, half).start()

                else:
                    exchange(index, half).start()
        if remote and index in LATE_HOLDS:

            @pl.when(late == 0)
            def _(index=index):
                exchange(index).start()

        elif index != CROSSING:
            exchange(index).start()

    if remote:

        @pl.when(late == 1)
        def _():
            for index in LATE_HOLDS:
                exchange(index).start()

    for copy in staged_late:
        copy.wait()

    for d in range(3):
        for h in range(4):
            nodes[6 * d + 1 + h] = jnp.broadcast_to(node_vel[d, h : h + 1, :], (8, CB))

    def corners(tile):
        for corner in range(4):
            at = face_nodes[pl.ds(tile * 32 + corner, 8, stride=4), :]
            yield at & 127, at >> 7

    def inner_sweep(tile):
        sums = [0.0] * 3
        for lanes, chunk in corners(tile):
            masks = [chunk == h for h in range(1, 5)]
            for d in range(3):
                value = 0.0
                for h in range(1, 5):
                    value = jnp.where(masks[h - 1], take(nodes[6 * d + h], lanes), value)
                sums[d] = sums[d] + value
        sweeps[rows8(tile), :] = dot3(normal_of(tile), sums)

    def outer_sweep(tile):
        sums = [0.0] * 3
        for lanes, chunk in corners(tile):
            below, above = chunk == 0, chunk == 5
            for d in range(3):
                value = jnp.where(below, take(nodes[6 * d], lanes), 0.0)
                sums[d] = sums[d] + jnp.where(above, take(nodes[6 * d + 5], lanes), value)
        total = sweeps[rows8(tile), :] + dot3(normal_of(tile), sums)
        sweeps[rows8(tile), :] = (0.25 * STEP_SIZE) * total

    def inner_tiles(t, _):
        for i in range(5):
            inner_sweep(5 * t + i)
        return 0

    lax.fori_loop(0, TILES // 5, inner_tiles, 0)

    for side in range(2):
        if remote:
            receives = has_nxt if side else has_prv

            @pl.when(receives == 1)
            def _(side=side):
                halo_copy(side).wait_recv()

        else:
            halo_copy(side).wait()
        for d in range(3):
            nodes[6 * d + 5 * side] = jnp.broadcast_to(halo[side, d : d + 1, :], (8, CB))
    if remote:
        for what in range(3):
            cross(what)

    for tile in [0] + [1 + RT * FLUX_ORDER[0] + t for t in range(RT)]:
        outer_sweep(tile)

    total[...] = jnp.zeros_like(total)
    split[...] = jnp.zeros_like(split)

    normal = normal_of(0)
    sweep = sweeps[0:8, :]
    left_cells = inner_cells[pl.ds(0, 8, stride=2), :]
    right_cells = inner_cells[pl.ds(1, 8, stride=2), :]
    left = rebuild(table, split_cells(left_cells), normal)
    right = rebuild(table, split_cells(right_cells), [-x for x in normal])
    flux = roe_flux(left, right, normal, sweep)
    scatter([-x for x in flux] + [sweep], left_cells, split.at[0], total)
    scatter(flux + [-sweep], right_cells, split.at[1], total)

    for place, index in enumerate(FLUX_ORDER):
        later = FLUX_ORDER[place + 1] if place + 1 < ROUNDS else None

        def flux_tile(pair, half, index=index):
            tile = 1 + RT * index + 2 * pair + half
            ours = [own[2 * index + pair, v, rows8(half), :] for v in range(5)]
            other = [theirs[2 * index + pair, v, rows8(half), :] for v in range(5)]
            sweep = sweeps[rows8(tile), :]
            flux = roe_flux(ours, other, normal_of(tile), sweep)
            scatter([-x for x in flux] + [sweep], cells_of(index, 2 * pair + half), split.at[half], total)

        def flux_pair(pair, _, later=later):
            if later is not None:
                for i in range(2):
                    outer_sweep(1 + RT * later + 2 * pair + i)
            flux_tile(pair, 0)
            flux_tile(pair, 1)
            return 0

        if index == CROSSING:
            for pair in range(2):
                exchange(CROSSING, pair).wait()
                flux_pair(pair, 0)
        else:
            exchange(index).wait()
            lax.fori_loop(0, RT // 2, flux_pair, 0)

    if remote:

        @pl.when(has_nxt == 1)
        def _():
            halo_copy(0).wait_send()

        @pl.when(has_prv == 1)
        def _():
            halo_copy(1).wait_send()


def finish(total, state, volume, counts, content, new_volume):
    live = jnp.broadcast_to(counts[...], (8, CB))
    for h in range(4):
        on = live > h
        sums = total[h * 16 : h * 16 + 6, :] + total[h * 16 + 6 : h * 16 + 12, :]
        room = volume[h : h + 1, :]
        content[:, h, :] = room * state[:, h, :] + jnp.where(on[0:5], STEP_SIZE * sums[0:5, :], 0.0)
        new_volume[h : h + 1, :] = room + jnp.where(on[0:1], sums[5:6, :], 0.0)


def section(remote, state, grad, adjacency, node_vel, face_normal, face_nodes, inner_cells, iface_cells, volume, counts):
    vmem = pl.BlockSpec(memory_space=pltpu.VMEM)
    hbm = pl.BlockSpec(memory_space=pltpu.HBM)
    params = dict(vmem_limit_bytes=VMEM_LIMIT)
    if remote:
        params.update(collective_id=0, has_side_effects=True)
    inputs = (state, grad, adjacency, node_vel, face_normal, face_nodes, inner_cells, iface_cells)
    total = pl.pallas_call(
        functools.partial(kernel, remote),
        out_shape=jax.ShapeDtypeStruct((64, CB), F32),
        in_specs=[hbm] * 8,
        out_specs=vmem,
        scratch_shapes=[
            *(pltpu.VMEM(x.shape, x.dtype) for x in inputs),
            pltpu.VMEM((80, 8, CB), F32),
            pltpu.VMEM((18, 8, CB), F32),
            pltpu.VMEM((2 * ROUNDS, 5, RT * 4, CB), F32),
            pltpu.VMEM((2 * ROUNDS, 5, RT * 4, CB), F32),
            pltpu.VMEM((TILES * 8, CB), F32),
            pltpu.VMEM((2, 3, HN), F32),
            pltpu.VMEM((2, 8 * RS, CB), F32),
            pltpu.SemaphoreType.DMA((2 * ROUNDS,)),
            pltpu.SemaphoreType.DMA((2 * ROUNDS,)),
            pltpu.SemaphoreType.DMA((2,)),
            pltpu.SemaphoreType.DMA((2,)),
            pltpu.SemaphoreType.DMA((11,)),
            pltpu.SemaphoreType.DMA((NB,)),
            pltpu.SemaphoreType.REGULAR((3,)),
        ],
        compiler_params=pltpu.CompilerParams(**params),
    )(*inputs)
    return pl.pallas_call(
        finish,
        out_shape=(
            jax.ShapeDtypeStruct((5, NB, CB), F32),
            jax.ShapeDtypeStruct((NB, CB), F32),
        ),
        in_specs=[vmem] * 4,
        out_specs=(vmem, vmem),
    )(total, state, volume, counts)


def by_chunk(rows):
    count, length = rows.shape
    return rows.reshape(count, length // CB, CB).swapaxes(0, 1).reshape(count * length // CB, CB)


def shards(
    state,
    grad_op,
    adjacency,
    node_vel,
    face_normal,
    face_nodes,
    inner_cells,
    iface_cells,
    cell_volume,
    block_counts,
):
    content, new_volume = section(
        True,
        state.reshape(5, NB, CB),
        grad_op.reshape(NB, K, CB, 3 * CB),
        jnp.swapaxes(adjacency, 2, 3).reshape(K, 1, NB),
        node_vel.reshape(3, NB, CB),
        face_normal.reshape(3, TILES * 8, CB),
        by_chunk(face_nodes[0, 0]),
        by_chunk(inner_cells[0, 0]),
        iface_cells.reshape(ROUNDS, RT * 8, CB),
        cell_volume.reshape(NB, CB),
        block_counts,
    )
    return (content.reshape(1, 1, 5, NN), new_volume.reshape(1, 1, NN))


def solution(mesh):
    return jax.shard_map(
        shards,
        mesh=mesh,
        in_specs=(
            P("zone", "dom", None, None),
            P("zone", "dom", None, None, None, None),
            P("zone", "dom", None, None),
            P("zone", "dom", None, None),
            P("zone", "dom", None, None),
            P("zone", "dom", None, None),
            P("zone", "dom", None, None),
            P("zone", "dom", None, None),
            P("zone", "dom", None),
            P("zone", "dom"),
        ),
        out_specs=(P("zone", "dom", None, None), P("zone", "dom", None)),
        check_vma=False,
    )
```

```python
import functools

import jax
import jax.numpy as jnp
from jax import lax
from jax.experimental import pallas as pl
from jax.experimental.pallas import tpu as pltpu
from jax.sharding import PartitionSpec as P

CB = 128
NB = 4
K = 3
ROUNDS = 6
HN = 128
NN = 512
RT = 4
TILES = 25
RS = 24

STEP_SIZE = 0.25
RECON_GAIN = 0.2
GAMMA_LESS = 0.4

LATE_ORDER = (2, 5, 3, 0, 4, 1)
EARLY_ORDER = (1, 4, 5, 3, 0, 2)
FLUX_ORDER = (0, 3, 5, 4)

REST_AFTER = 1
CROSSING = 2
HELD = 1
HOLD = 3
VMEM_LIMIT = 60 << 20

F32 = jnp.float32
BF16 = jnp.bfloat16


def take(row, lanes):
    return jnp.take_along_axis(row, lanes, axis=1, mode="promise_in_bounds")


def rows8(tile):
    return pl.ds(pl.multiple_of(tile * 8, 8), 8)


def split_cells(cells):
    return cells & 127, (cells & 128) != 0, (cells & 256) != 0


def pick(table, first, where):
    lanes, odd, upper = where
    low = jnp.where(odd, take(table[first + 1], lanes), take(table[first], lanes))
    high = jnp.where(odd, take(table[first + 3], lanes), take(table[first + 2], lanes))
    return jnp.where(upper, high, low)


def rebuild(table, where, normal):
    cons = [pick(table, 4 * v, where) for v in range(5)]
    delta = []
    for v in range(5):
        parts = [pick(table, 20 + 4 * (3 * v + d), where) * normal[d] for d in range(3)]
        delta.append(parts[0] + parts[1] + parts[2])
    per_dens = 1.0 / cons[0]
    gain = RECON_GAIN * cons[0]
    out = [cons[0] + gain * jnp.tanh(delta[0] * per_dens)]
    for v in range(1, 4):
        out.append(cons[v] + gain * jnp.tanh(delta[v] * per_dens))
    out.append(cons[4] + RECON_GAIN * cons[4] * jnp.tanh(delta[4] / cons[4]))
    return out


def dot3(a, b):
    return a[0] * b[0] + a[1] * b[1] + a[2] * b[2]


def side_values(cons, unit):
    per_dens = 1.0 / cons[0]
    vel = [cons[i] * per_dens for i in (1, 2, 3)]
    pres = GAMMA_LESS * (cons[4] - 0.5 * dot3(cons[1:4], vel))
    enth = (cons[4] + pres) * per_dens
    return vel, pres, enth, dot3(vel, unit)


def roe_flux(left, right, normal, sweep):
    area_sq = dot3(normal, normal)
    per_area = lax.rsqrt(area_sq)
    area = area_sq * per_area
    unit = [x * per_area for x in normal]
    grid = sweep * per_area * (1.0 / STEP_SIZE)
    vel_l, pres_l, enth_l, q_l = side_values(left, unit)
    vel_r, pres_r, enth_r, q_r = side_values(right, unit)
    root_l = jnp.sqrt(left[0])
    root_r = jnp.sqrt(right[0])
    per_sum = 1.0 / (root_l + root_r)
    a = root_l * per_sum
    b = root_r * per_sum
    vel = [a * x + b * y for x, y in zip(vel_l, vel_r)]
    enth = a * enth_l + b * enth_r
    dens = root_l * root_r
    q = dot3(vel, unit)
    kinetic = 0.5 * dot3(vel, vel)
    c_sq = GAMMA_LESS * (enth - kinetic)
    c = jnp.sqrt(c_sq)
    per_c_sq = 1.0 / c_sq
    d_pres = pres_r - pres_l
    d_dens = right[0] - left[0]
    d_vel = [y - x for x, y in zip(vel_l, vel_r)]
    d_q = dot3(d_vel, unit)
    fix = 0.01 * c_sq
    rel = q - grid
    slow = rel - c
    fast = rel + c
    wave_slow = jnp.sqrt(slow * slow + fix)
    wave_mid = jnp.sqrt(rel * rel + fix)
    wave_fast = jnp.sqrt(fast * fast + fix)
    half = 0.5 * per_c_sq
    cross = dens * c * d_q
    part_slow = wave_slow * ((d_pres - cross) * half)
    part_fast = wave_fast * ((d_pres + cross) * half)
    part_mid = wave_mid * (d_dens - d_pres * per_c_sq)
    shear = wave_mid * dens
    both = part_slow + part_fast
    total = both + part_mid
    diff = c * (part_fast - part_slow)
    move_l = q_l - grid
    move_r = q_r - grid
    along = pres_l + pres_r - diff + shear * d_q
    out = [left[0] * move_l + right[0] * move_r - total]
    for i in range(3):
        out.append(
            left[i + 1] * move_l
            + right[i + 1] * move_r
            + along * unit[i]
            - total * vel[i]
            - shear * d_vel[i]
        )
    out.append(
        left[4] * move_l
        + right[4] * move_r
        + pres_l * q_l
        + pres_r * q_r
        - both * enth
        - diff * q
        - part_mid * kinetic
        - shear * (dot3(vel, d_vel) - q * d_q)
    )
    scale = 0.5 * area
    return [scale * x for x in out]


def scatter(terms, where_cells, split, total):
    for v, x in enumerate(terms):
        upper = x.astype(BF16).astype(F32)
        split[pl.ds(v, 8, stride=RS), :] = upper
        split[pl.ds(v + 6, 8, stride=RS), :] = x - upper
    lanes = (where_cells & 127).astype(F32)
    chunk = (where_cells >> 7).astype(F32)
    slot = lax.broadcasted_iota(jnp.int32, (CB, CB), 0).astype(F32).astype(BF16)
    one, zero = jnp.ones((), BF16), jnp.zeros((), BF16)
    result = None
    for s in range(0, 8, 2):
        left, right = [], []
        for i in (s, s + 1):
            rows = split[i * RS : i * RS + 16, :].astype(BF16)
            home = jnp.broadcast_to(chunk[i : i + 1, :], (16, CB)).astype(BF16)
            left.append(jnp.concatenate([jnp.where(home == h, rows, zero) for h in range(4)], axis=0))
            at = jnp.broadcast_to(lanes[i : i + 1, :], (CB, CB)).astype(BF16)
            right.append(jnp.where(at == slot, one, zero))
        left, right = jnp.concatenate(left, axis=1), jnp.concatenate(right, axis=1)
        part = lax.dot_general(left, right, (((1,), (1,)), ((), ())), preferred_element_type=F32)
        result = part if result is None else result + part
    total[...] += result


def kernel(
    remote,
    state_hbm,
    grad_hbm,
    adjacency_hbm,
    node_vel_hbm,
    face_normal_hbm,
    face_nodes_hbm,
    inner_cells_hbm,
    iface_cells_hbm,
    total,
    state,
    grad,
    adjacency,
    node_vel,
    face_normal,
    face_nodes,
    inner_cells,
    iface_cells,
    table,
    nodes,
    own,
    theirs,
    sweeps,
    halo,
    split,
    send_sem,
    recv_sem,
    halo_send,
    halo_recv,
    stage_sem,
    grad_sem,
    ready,
):
    def stage(source, target, sem):
        copy = pltpu.make_async_copy(source, target, sem)
        copy.start()
        return copy

    halo[...] = jnp.zeros_like(halo)
    staged_state = stage(state_hbm, state, stage_sem.at[0])
    staged_adjacency = stage(adjacency_hbm, adjacency, stage_sem.at[1])
    staged_grad = [stage(grad_hbm.at[b], grad.at[b], grad_sem.at[b]) for b in range(NB)]
    staged_first = [
        stage(iface_cells_hbm, iface_cells, stage_sem.at[2]),
        stage(face_normal_hbm, face_normal, stage_sem.at[3]),
    ]

    def stage_rest():
        return [
            stage(node_vel_hbm, node_vel, stage_sem.at[4]),
            stage(inner_cells_hbm, inner_cells, stage_sem.at[5]),
            stage(face_nodes_hbm, face_nodes, stage_sem.at[6]),
        ]

    if remote:
        zone = lax.axis_index("zone")
        dom = lax.axis_index("dom")
        n_dom = lax.axis_size("dom")
        nxt = lax.rem(dom + 1, n_dom)
        prv = lax.rem(dom + n_dom - 1, n_dom)
        has_nxt = 1 - (dom + 1) // n_dom
        has_prv = 1 - (n_dom - dom) // n_dom

        def flip(at, bit):
            return at + bit * (1 - 2 * ((at // bit) % 2))

        peers = [
            (zone, flip(dom, 1)),
            (zone, flip(dom, 2)),
            (zone, flip(dom, 4)),
            (zone, flip(dom, 8)),
            (flip(zone, 1), dom),
            (zone, flip(dom, 16)),
        ]
        def is_late(at):
            return (at // 4) % 2

        late = is_late(dom)
        early = 1 - late
        late_nxt = is_late(nxt)
        late_prv = is_late(prv)

        def signal(sem, peer):
            pl.semaphore_signal(sem, inc=1, device_id=peer, device_id_type=pl.DeviceIdType.MESH)

        barrier = pltpu.get_barrier_semaphore()
        for index in (4, 1, 0, 3, 5):
            signal(barrier, peers[index])

        @pl.when(early == 1)
        def _():
            signal(barrier, peers[2])

        @pl.when(has_nxt * (early + late_nxt) > 0)
        def _():
            signal(barrier, (zone, nxt))

        @pl.when(has_prv * (early + late_prv) > 0)
        def _():
            signal(barrier, (zone, prv))

    def exchange(index, half=None):
        if half is None:
            at, sem = pl.ds(2 * index, 2), 2 * index
        else:
            at = sem = 2 * index + half
        if remote:
            return pltpu.make_async_remote_copy(
                src_ref=own.at[at],
                dst_ref=theirs.at[at],
                send_sem=send_sem.at[sem],
                recv_sem=recv_sem.at[sem],
                device_id=peers[index],
                device_id_type=pl.DeviceIdType.MESH,
            )
        return pltpu.make_async_copy(own.at[at], theirs.at[at], recv_sem.at[sem])

    def halo_copy(side):
        source = node_vel_hbm.at[:, 3 * (1 - side), :]
        if remote:
            return pltpu.make_async_remote_copy(
                src_ref=source,
                dst_ref=halo.at[side],
                send_sem=halo_send.at[side],
                recv_sem=halo_recv.at[side],
                device_id=(zone, prv if side else nxt),
                device_id_type=pl.DeviceIdType.MESH,
            )
        return pltpu.make_async_copy(source, halo.at[side], halo_recv.at[side])

    def enter():
        meet_nxt = has_nxt * (1 - early * late_nxt)
        meet_prv = has_prv * (1 - early * late_prv)
        pl.semaphore_wait(barrier, 5 + late + meet_nxt + meet_prv)

        @pl.when(late == 1)
        def _():
            signal(ready.at[0], peers[2])

        @pl.when(late * (1 - late_nxt) * has_nxt == 1)
        def _():
            signal(ready.at[1], (zone, nxt))

        @pl.when(late * (1 - late_prv) * has_prv == 1)
        def _():
            signal(ready.at[2], (zone, prv))

        @pl.when(meet_nxt == 1)
        def _():
            halo_copy(0).start()

        @pl.when(meet_prv == 1)
        def _():
            halo_copy(1).start()

    def cross(what):
        if what == 0:

            @pl.when(early * late_nxt * has_nxt == 1)
            def _():
                pl.semaphore_wait(ready.at[2], 1)
                halo_copy(0).start()

        elif what == 1:

            @pl.when(early * late_prv * has_prv == 1)
            def _():
                pl.semaphore_wait(ready.at[1], 1)
                halo_copy(1).start()

        else:
            mixed = late_nxt * has_nxt + late_prv * has_prv

            @pl.when(early * (mixed if what == 2 else 1 - mixed) == 1)
            def _():
                pl.semaphore_wait(ready.at[0], 1)
                for half in range(2):
                    exchange(CROSSING, half).start()

    if remote:
        pl.when(late == 1)(enter)

    staged_state.wait()
    staged_adjacency.wait()
    for v in range(5):
        for h in range(4):
            table[4 * v + h] = jnp.broadcast_to(state[v, h : h + 1, :], (8, CB))
    for b in range(NB):
        sums = None
        staged_grad[b].wait()
        if b == REST_AFTER:
            staged_late = stage_rest()
        for k in range(K):
            near = jnp.broadcast_to(adjacency[k, :, b : b + 1], (5, CB))
            block = state[:, 0, :]
            for other in range(1, NB):
                block = jnp.where(near == other, state[:, other, :], block)
            part = jnp.dot(block.astype(BF16), grad[b, k], preferred_element_type=F32)
            sums = part if sums is None else sums + part
        for v in range(5):
            for d in range(3):
                table[20 + 4 * (3 * v + d) + b] = jnp.broadcast_to(
                    sums[v : v + 1, d * CB : (d + 1) * CB], (8, CB)
                )

    def normal_of(tile):
        return [face_normal[d, rows8(tile), :] for d in range(3)]

    def cells_of(index, t):
        return iface_cells[index, rows8(t), :]

    if remote:
        pl.when(early == 1)(enter)
    else:
        for side in range(2):
            halo_copy(side).start()

    for copy in staged_first:
        copy.wait()

    for place in range(ROUNDS):
        late_index, early_index = LATE_ORDER[place], EARLY_ORDER[place]
        index = late_index * late + early_index * (1 - late) if remote else late_index
        for half in range(2):
            for t in range(2):
                tile = 2 * half + t
                where = split_cells(cells_of(index, tile))
                out = rebuild(table, where, normal_of(1 + RT * index + tile))
                for v in range(5):
                    own[2 * index + half, v, rows8(t), :] = out[v]
            if late_index == CROSSING:
                if remote:

                    @pl.when(late == 1)
                    def _(half=half):
                        exchange(CROSSING, half).start()

                else:
                    exchange(CROSSING, half).start()
        if remote:
            if late_index not in (CROSSING, HELD):

                @pl.when(late == 1)
                def _(index=late_index):
                    exchange(index).start()

            if early_index != CROSSING:

                @pl.when(late == 0)
                def _(index=early_index):
                    for half in (0, 1) if index == HELD else (None,):
                        exchange(index, half).start()

        elif late_index == HELD:
            for half in range(2):
                exchange(HELD, half).start()
        elif late_index != CROSSING:
            exchange(late_index).start()

    for copy in staged_late:
        copy.wait()

    for d in range(3):
        for h in range(4):
            nodes[6 * d + 1 + h] = jnp.broadcast_to(node_vel[d, h : h + 1, :], (8, CB))

    def corners(tile):
        for corner in range(4):
            at = face_nodes[pl.ds(tile * 32 + corner, 8, stride=4), :]
            yield at & 127, at >> 7

    def inner_sweep(tile):
        sums = [0.0] * 3
        for lanes, chunk in corners(tile):
            masks = [chunk == h for h in range(1, 5)]
            for d in range(3):
                value = 0.0
                for h in range(1, 5):
                    value = jnp.where(masks[h - 1], take(nodes[6 * d + h], lanes), value)
                sums[d] = sums[d] + value
        sweeps[rows8(tile), :] = dot3(normal_of(tile), sums)

    def outer_sweep(tile):
        sums = [0.0] * 3
        for lanes, chunk in corners(tile):
            below, above = chunk == 0, chunk == 5
            for d in range(3):
                value = jnp.where(below, take(nodes[6 * d], lanes), 0.0)
                sums[d] = sums[d] + jnp.where(above, take(nodes[6 * d + 5], lanes), value)
        total = sweeps[rows8(tile), :] + dot3(normal_of(tile), sums)
        sweeps[rows8(tile), :] = (0.25 * STEP_SIZE) * total

    def inner_tiles(t, _):
        for i in range(5):
            inner_sweep(5 * t + i)
        return 0

    lax.fori_loop(0, HOLD, inner_tiles, 0)
    if remote:

        @pl.when(late == 1)
        def _():
            for half in range(2):
                exchange(HELD, half).start()

    lax.fori_loop(HOLD, TILES // 5, inner_tiles, 0)

    for side in range(2):
        if remote:
            receives = has_nxt if side else has_prv

            @pl.when(receives == 1)
            def _(side=side):
                halo_copy(side).wait_recv()

        else:
            halo_copy(side).wait()
        for d in range(3):
            nodes[6 * d + 5 * side] = jnp.broadcast_to(halo[side, d : d + 1, :], (8, CB))
    if remote:
        for what in range(3):
            cross(what)

    for tile in [0] + [1 + RT * FLUX_ORDER[0] + t for t in range(RT)]:
        outer_sweep(tile)

    total[...] = jnp.zeros_like(total)
    split[...] = jnp.zeros_like(split)

    normal = normal_of(0)
    sweep = sweeps[0:8, :]
    left_cells = inner_cells[pl.ds(0, 8, stride=2), :]
    right_cells = inner_cells[pl.ds(1, 8, stride=2), :]
    left = rebuild(table, split_cells(left_cells), normal)
    right = rebuild(table, split_cells(right_cells), [-x for x in normal])
    flux = roe_flux(left, right, normal, sweep)
    scatter([-x for x in flux] + [sweep], left_cells, split.at[0], total)
    scatter(flux + [-sweep], right_cells, split.at[1], total)

    early_order, late_order = FLUX_ORDER + (HELD, CROSSING), FLUX_ORDER + (CROSSING, HELD)

    def at_place(place):
        if not remote or early_order[place] == late_order[place]:
            return early_order[place]
        return late_order[place] * late + early_order[place] * (1 - late)

    for place in range(ROUNDS):
        index = at_place(place)
        later = at_place(place + 1) if place + 1 < ROUNDS else None
        if remote and place == 1:
            cross(3)

        def flux_tile(pair, half, index=index):
            tile = 1 + RT * index + 2 * pair + half
            ours = [own[2 * index + pair, v, rows8(half), :] for v in range(5)]
            other = [theirs[2 * index + pair, v, rows8(half), :] for v in range(5)]
            sweep = sweeps[rows8(tile), :]
            flux = roe_flux(ours, other, normal_of(tile), sweep)
            scatter([-x for x in flux] + [sweep], cells_of(index, 2 * pair + half), split.at[half], total)

        def flux_pair(pair, _, later=later):
            if later is not None:
                for i in range(2):
                    outer_sweep(1 + RT * later + 2 * pair + i)
            flux_tile(pair, 0)
            flux_tile(pair, 1)
            return 0

        if early_order[place] in (HELD, CROSSING):
            for pair in range(2):
                if remote:
                    for side, order in ((0, early_order), (1, late_order)):

                        @pl.when(late == side)
                        def _(index=order[place], pair=pair):
                            exchange(index, pair).wait()

                else:
                    exchange(index, pair).wait()
                flux_pair(pair, 0)
        else:
            exchange(index).wait()
            lax.fori_loop(0, RT // 2, flux_pair, 0)

    if remote:

        @pl.when(has_nxt == 1)
        def _():
            halo_copy(0).wait_send()

        @pl.when(has_prv == 1)
        def _():
            halo_copy(1).wait_send()


def finish(total, state, volume, counts, content, new_volume):
    live = jnp.broadcast_to(counts[...], (8, CB))
    for h in range(4):
        on = live > h
        sums = total[h * 16 : h * 16 + 6, :] + total[h * 16 + 6 : h * 16 + 12, :]
        room = volume[h : h + 1, :]
        content[:, h, :] = room * state[:, h, :] + jnp.where(on[0:5], STEP_SIZE * sums[0:5, :], 0.0)
        new_volume[h : h + 1, :] = room + jnp.where(on[0:1], sums[5:6, :], 0.0)


def section(remote, state, grad, adjacency, node_vel, face_normal, face_nodes, inner_cells, iface_cells, volume, counts):
    vmem = pl.BlockSpec(memory_space=pltpu.VMEM)
    hbm = pl.BlockSpec(memory_space=pltpu.HBM)
    params = dict(vmem_limit_bytes=VMEM_LIMIT)
    if remote:
        params.update(collective_id=0, has_side_effects=True)
    inputs = (state, grad, adjacency, node_vel, face_normal, face_nodes, inner_cells, iface_cells)
    total = pl.pallas_call(
        functools.partial(kernel, remote),
        out_shape=jax.ShapeDtypeStruct((64, CB), F32),
        in_specs=[hbm] * 8,
        out_specs=vmem,
        scratch_shapes=[
            *(pltpu.VMEM(x.shape, x.dtype) for x in inputs),
            pltpu.VMEM((80, 8, CB), F32),
            pltpu.VMEM((18, 8, CB), F32),
            pltpu.VMEM((2 * ROUNDS, 5, RT * 4, CB), F32),
            pltpu.VMEM((2 * ROUNDS, 5, RT * 4, CB), F32),
            pltpu.VMEM((TILES * 8, CB), F32),
            pltpu.VMEM((2, 3, HN), F32),
            pltpu.VMEM((2, 8 * RS, CB), F32),
            pltpu.SemaphoreType.DMA((2 * ROUNDS,)),
            pltpu.SemaphoreType.DMA((2 * ROUNDS,)),
            pltpu.SemaphoreType.DMA((2,)),
            pltpu.SemaphoreType.DMA((2,)),
            pltpu.SemaphoreType.DMA((7,)),
            pltpu.SemaphoreType.DMA((NB,)),
            pltpu.SemaphoreType.REGULAR((3,)),
        ],
        compiler_params=pltpu.CompilerParams(**params),
    )(*inputs)
    return pl.pallas_call(
        finish,
        out_shape=(
            jax.ShapeDtypeStruct((5, NB, CB), F32),
            jax.ShapeDtypeStruct((NB, CB), F32),
        ),
        in_specs=[vmem] * 4,
        out_specs=(vmem, vmem),
    )(total, state, volume, counts)


def by_chunk(rows):
    count, length = rows.shape
    return rows.reshape(count, length // CB, CB).swapaxes(0, 1).reshape(count * length // CB, CB)


def shards(
    state,
    grad_op,
    adjacency,
    node_vel,
    face_normal,
    face_nodes,
    inner_cells,
    iface_cells,
    cell_volume,
    block_counts,
):
    content, new_volume = section(
        True,
        state.reshape(5, NB, CB),
        grad_op.reshape(NB, K, CB, 3 * CB),
        jnp.swapaxes(adjacency, 2, 3).reshape(K, 1, NB),
        node_vel.reshape(3, NB, CB),
        face_normal.reshape(3, TILES * 8, CB),
        by_chunk(face_nodes[0, 0]),
        by_chunk(inner_cells[0, 0]),
        iface_cells.reshape(ROUNDS, RT * 8, CB),
        cell_volume.reshape(NB, CB),
        block_counts,
    )
    return (content.reshape(1, 1, 5, NN), new_volume.reshape(1, 1, NN))


def solution(mesh):
    return jax.shard_map(
        shards,
        mesh=mesh,
        in_specs=(
            P("zone", "dom", None, None),
            P("zone", "dom", None, None, None, None),
            P("zone", "dom", None, None),
            P("zone", "dom", None, None),
            P("zone", "dom", None, None),
            P("zone", "dom", None, None),
            P("zone", "dom", None, None),
            P("zone", "dom", None, None),
            P("zone", "dom", None),
            P("zone", "dom"),
        ),
        out_specs=(P("zone", "dom", None, None), P("zone", "dom", None)),
        check_vma=False,
    )
```

```python
import functools

import jax
import jax.numpy as jnp
from jax import lax
from jax.experimental import pallas as pl
from jax.experimental.pallas import tpu as pltpu
from jax.sharding import PartitionSpec as P

CB = 128
NB = 4
K = 3
ROUNDS = 6
HN = 128
NN = 512
RT = 4
TILES = 25
RS = 24

STEP_SIZE = 0.25
RECON_GAIN = 0.2
GAMMA_LESS = 0.4

LATE_ORDER = (2, 5, 3, 0, 4, 1)
EARLY_ORDER = (1, 4, 5, 3, 0, 2)
FLUX_ORDER = (0, 3, 5, 4)

REST_AFTER = 1
CROSSING = 2
HELD = 1
HOLD = 3
VMEM_LIMIT = 60 << 20

F32 = jnp.float32
BF16 = jnp.bfloat16


def take(row, lanes):
    return jnp.take_along_axis(row, lanes, axis=1, mode="promise_in_bounds")


def rows8(tile):
    return pl.ds(pl.multiple_of(tile * 8, 8), 8)


def split_cells(cells):
    return cells & 127, (cells & 128) != 0, (cells & 256) != 0


def pick(table, first, where):
    lanes, odd, upper = where
    low = jnp.where(odd, take(table[first + 1], lanes), take(table[first], lanes))
    high = jnp.where(odd, take(table[first + 3], lanes), take(table[first + 2], lanes))
    return jnp.where(upper, high, low)


def rebuild(table, where, normal):
    cons = [pick(table, 4 * v, where) for v in range(5)]
    delta = []
    for v in range(5):
        parts = [pick(table, 20 + 4 * (3 * v + d), where) * normal[d] for d in range(3)]
        delta.append(parts[0] + parts[1] + parts[2])
    per_dens = 1.0 / cons[0]
    gain = RECON_GAIN * cons[0]
    out = [cons[0] + gain * jnp.tanh(delta[0] * per_dens)]
    for v in range(1, 4):
        out.append(cons[v] + gain * jnp.tanh(delta[v] * per_dens))
    out.append(cons[4] + RECON_GAIN * cons[4] * jnp.tanh(delta[4] / cons[4]))
    return out


def dot3(a, b):
    return a[0] * b[0] + a[1] * b[1] + a[2] * b[2]


def side_values(cons, unit):
    per_dens = 1.0 / cons[0]
    vel = [cons[i] * per_dens for i in (1, 2, 3)]
    pres = GAMMA_LESS * (cons[4] - 0.5 * dot3(cons[1:4], vel))
    enth = (cons[4] + pres) * per_dens
    return vel, pres, enth, dot3(vel, unit)


def roe_flux(left, right, normal, sweep):
    area_sq = dot3(normal, normal)
    per_area = lax.rsqrt(area_sq)
    area = area_sq * per_area
    unit = [x * per_area for x in normal]
    grid = sweep * per_area * (1.0 / STEP_SIZE)
    vel_l, pres_l, enth_l, q_l = side_values(left, unit)
    vel_r, pres_r, enth_r, q_r = side_values(right, unit)
    root_l = jnp.sqrt(left[0])
    root_r = jnp.sqrt(right[0])
    per_sum = 1.0 / (root_l + root_r)
    a = root_l * per_sum
    b = root_r * per_sum
    vel = [a * x + b * y for x, y in zip(vel_l, vel_r)]
    enth = a * enth_l + b * enth_r
    dens = root_l * root_r
    q = dot3(vel, unit)
    kinetic = 0.5 * dot3(vel, vel)
    c_sq = GAMMA_LESS * (enth - kinetic)
    c = jnp.sqrt(c_sq)
    per_c_sq = 1.0 / c_sq
    d_pres = pres_r - pres_l
    d_dens = right[0] - left[0]
    d_vel = [y - x for x, y in zip(vel_l, vel_r)]
    d_q = dot3(d_vel, unit)
    fix = 0.01 * c_sq
    rel = q - grid
    slow = rel - c
    fast = rel + c
    wave_slow = jnp.sqrt(slow * slow + fix)
    wave_mid = jnp.sqrt(rel * rel + fix)
    wave_fast = jnp.sqrt(fast * fast + fix)
    half = 0.5 * per_c_sq
    cross = dens * c * d_q
    part_slow = wave_slow * ((d_pres - cross) * half)
    part_fast = wave_fast * ((d_pres + cross) * half)
    part_mid = wave_mid * (d_dens - d_pres * per_c_sq)
    shear = wave_mid * dens
    both = part_slow + part_fast
    total = both + part_mid
    diff = c * (part_fast - part_slow)
    move_l = q_l - grid
    move_r = q_r - grid
    along = pres_l + pres_r - diff + shear * d_q
    out = [left[0] * move_l + right[0] * move_r - total]
    for i in range(3):
        out.append(
            left[i + 1] * move_l
            + right[i + 1] * move_r
            + along * unit[i]
            - total * vel[i]
            - shear * d_vel[i]
        )
    out.append(
        left[4] * move_l
        + right[4] * move_r
        + pres_l * q_l
        + pres_r * q_r
        - both * enth
        - diff * q
        - part_mid * kinetic
        - shear * (dot3(vel, d_vel) - q * d_q)
    )
    scale = 0.5 * area
    return [scale * x for x in out]


def scatter(terms, where_cells, split, total):
    for v, x in enumerate(terms):
        upper = x.astype(BF16).astype(F32)
        split[pl.ds(v, 8, stride=RS), :] = upper
        split[pl.ds(v + 6, 8, stride=RS), :] = x - upper
    lanes = (where_cells & 127).astype(F32)
    chunk = (where_cells >> 7).astype(F32)
    slot = lax.broadcasted_iota(jnp.int32, (CB, CB), 0).astype(F32).astype(BF16)
    one, zero = jnp.ones((), BF16), jnp.zeros((), BF16)
    result = None
    for s in range(0, 8, 2):
        left, right = [], []
        for i in (s, s + 1):
            rows = split[i * RS : i * RS + 16, :].astype(BF16)
            home = jnp.broadcast_to(chunk[i : i + 1, :], (16, CB)).astype(BF16)
            left.append(jnp.concatenate([jnp.where(home == h, rows, zero) for h in range(4)], axis=0))
            at = jnp.broadcast_to(lanes[i : i + 1, :], (CB, CB)).astype(BF16)
            right.append(jnp.where(at == slot, one, zero))
        left, right = jnp.concatenate(left, axis=1), jnp.concatenate(right, axis=1)
        part = lax.dot_general(left, right, (((1,), (1,)), ((), ())), preferred_element_type=F32)
        result = part if result is None else result + part
    total[...] += result


def kernel(
    remote,
    state_hbm,
    grad_hbm,
    adjacency_hbm,
    node_vel_hbm,
    face_normal_hbm,
    face_nodes_hbm,
    inner_cells_hbm,
    iface_cells_hbm,
    total,
    state,
    grad,
    adjacency,
    node_vel,
    face_normal,
    face_nodes,
    inner_cells,
    iface_cells,
    table,
    nodes,
    own,
    theirs,
    sweeps,
    halo,
    split,
    send_sem,
    recv_sem,
    halo_send,
    halo_recv,
    stage_sem,
    grad_sem,
    ready,
    inner_sides,
):
    def stage(source, target, sem):
        copy = pltpu.make_async_copy(source, target, sem)
        copy.start()
        return copy

    halo[...] = jnp.zeros_like(halo)
    staged_state = stage(state_hbm, state, stage_sem.at[0])
    staged_adjacency = stage(adjacency_hbm, adjacency, stage_sem.at[1])
    staged_grad = [stage(grad_hbm.at[b], grad.at[b], grad_sem.at[b]) for b in range(NB)]
    staged_first = [
        stage(iface_cells_hbm, iface_cells, stage_sem.at[2]),
        stage(face_normal_hbm, face_normal, stage_sem.at[3]),
    ]

    def stage_rest():
        return [
            stage(node_vel_hbm, node_vel, stage_sem.at[4]),
            stage(inner_cells_hbm, inner_cells, stage_sem.at[5]),
            stage(face_nodes_hbm, face_nodes, stage_sem.at[6]),
        ]

    if remote:
        zone = lax.axis_index("zone")
        dom = lax.axis_index("dom")
        n_dom = lax.axis_size("dom")
        nxt = lax.rem(dom + 1, n_dom)
        prv = lax.rem(dom + n_dom - 1, n_dom)
        has_nxt = 1 - (dom + 1) // n_dom
        has_prv = 1 - (n_dom - dom) // n_dom

        def flip(at, bit):
            return at + bit * (1 - 2 * ((at // bit) % 2))

        peers = [
            (zone, flip(dom, 1)),
            (zone, flip(dom, 2)),
            (zone, flip(dom, 4)),
            (zone, flip(dom, 8)),
            (flip(zone, 1), dom),
            (zone, flip(dom, 16)),
        ]
        def is_late(at):
            return (at // 4) % 2

        late = is_late(dom)
        early = 1 - late
        late_nxt = is_late(nxt)
        late_prv = is_late(prv)

        def signal(sem, peer):
            pl.semaphore_signal(sem, inc=1, device_id=peer, device_id_type=pl.DeviceIdType.MESH)

        barrier = pltpu.get_barrier_semaphore()
        for index in (4, 1, 0, 3, 5):
            signal(barrier, peers[index])

        @pl.when(early == 1)
        def _():
            signal(barrier, peers[2])

        @pl.when(has_nxt * (early + late_nxt) > 0)
        def _():
            signal(barrier, (zone, nxt))

        @pl.when(has_prv * (early + late_prv) > 0)
        def _():
            signal(barrier, (zone, prv))

    def exchange(index, half=None):
        if half is None:
            at, sem = pl.ds(2 * index, 2), 2 * index
        else:
            at = sem = 2 * index + half
        if remote:
            return pltpu.make_async_remote_copy(
                src_ref=own.at[at],
                dst_ref=theirs.at[at],
                send_sem=send_sem.at[sem],
                recv_sem=recv_sem.at[sem],
                device_id=peers[index],
                device_id_type=pl.DeviceIdType.MESH,
            )
        return pltpu.make_async_copy(own.at[at], theirs.at[at], recv_sem.at[sem])

    def halo_copy(side):
        source = node_vel_hbm.at[:, 3 * (1 - side), :]
        if remote:
            return pltpu.make_async_remote_copy(
                src_ref=source,
                dst_ref=halo.at[side],
                send_sem=halo_send.at[side],
                recv_sem=halo_recv.at[side],
                device_id=(zone, prv if side else nxt),
                device_id_type=pl.DeviceIdType.MESH,
            )
        return pltpu.make_async_copy(source, halo.at[side], halo_recv.at[side])

    def enter():
        meet_nxt = has_nxt * (1 - early * late_nxt)
        meet_prv = has_prv * (1 - early * late_prv)
        pl.semaphore_wait(barrier, 5 + late + meet_nxt + meet_prv)

        @pl.when(late == 1)
        def _():
            signal(ready.at[0], peers[2])

        @pl.when(late * (1 - late_nxt) * has_nxt == 1)
        def _():
            signal(ready.at[1], (zone, nxt))

        @pl.when(late * (1 - late_prv) * has_prv == 1)
        def _():
            signal(ready.at[2], (zone, prv))

        @pl.when(meet_nxt == 1)
        def _():
            halo_copy(0).start()

        @pl.when(meet_prv == 1)
        def _():
            halo_copy(1).start()

    def cross(what):
        if what == 0:

            @pl.when(early * late_nxt * has_nxt == 1)
            def _():
                pl.semaphore_wait(ready.at[2], 1)
                halo_copy(0).start()

        elif what == 1:

            @pl.when(early * late_prv * has_prv == 1)
            def _():
                pl.semaphore_wait(ready.at[1], 1)
                halo_copy(1).start()

        else:
            mixed = late_nxt * has_nxt + late_prv * has_prv

            @pl.when(early * (mixed if what == 2 else 1 - mixed) == 1)
            def _():
                pl.semaphore_wait(ready.at[0], 1)
                for half in range(2):
                    exchange(CROSSING, half).start()

    staged_state.wait()
    staged_adjacency.wait()
    for v in range(5):
        for h in range(4):
            table[4 * v + h] = jnp.broadcast_to(state[v, h : h + 1, :], (8, CB))
    for b in range(NB):
        sums = None
        staged_grad[b].wait()
        if b == REST_AFTER:
            staged_late = stage_rest()
            if remote:
                pl.when(late == 1)(enter)
        for k in range(K):
            near = jnp.broadcast_to(adjacency[k, :, b : b + 1], (5, CB))
            block = state[:, 0, :]
            for other in range(1, NB):
                block = jnp.where(near == other, state[:, other, :], block)
            part = jnp.dot(block.astype(BF16), grad[b, k], preferred_element_type=F32)
            sums = part if sums is None else sums + part
        for v in range(5):
            for d in range(3):
                table[20 + 4 * (3 * v + d) + b] = jnp.broadcast_to(
                    sums[v : v + 1, d * CB : (d + 1) * CB], (8, CB)
                )

    def normal_of(tile):
        return [face_normal[d, rows8(tile), :] for d in range(3)]

    def cells_of(index, t):
        return iface_cells[index, rows8(t), :]

    if remote:
        pl.when(early == 1)(enter)
    else:
        for side in range(2):
            halo_copy(side).start()

    for copy in staged_first:
        copy.wait()

    for place in range(ROUNDS):
        late_index, early_index = LATE_ORDER[place], EARLY_ORDER[place]
        index = late_index * late + early_index * (1 - late) if remote else late_index
        for half in range(2):
            for t in range(2):
                tile = 2 * half + t
                where = split_cells(cells_of(index, tile))
                out = rebuild(table, where, normal_of(1 + RT * index + tile))
                for v in range(5):
                    own[2 * index + half, v, rows8(t), :] = out[v]
            if late_index == CROSSING:
                if remote:

                    @pl.when(late == 1)
                    def _(half=half):
                        exchange(CROSSING, half).start()

                else:
                    exchange(CROSSING, half).start()
        if remote:
            if late_index not in (CROSSING, HELD):

                @pl.when(late == 1)
                def _(index=late_index):
                    exchange(index).start()

            if early_index != CROSSING:

                @pl.when(late == 0)
                def _(index=early_index):
                    for half in (0, 1) if index == HELD else (None,):
                        exchange(index, half).start()

        elif late_index == HELD:
            for half in range(2):
                exchange(HELD, half).start()
        elif late_index != CROSSING:
            exchange(late_index).start()

    for copy in staged_late:
        copy.wait()

    for d in range(3):
        for h in range(4):
            nodes[6 * d + 1 + h] = jnp.broadcast_to(node_vel[d, h : h + 1, :], (8, CB))

    def corners(tile):
        for corner in range(4):
            at = face_nodes[pl.ds(tile * 32 + corner, 8, stride=4), :]
            yield at & 127, at >> 7

    def inner_sweep(tile):
        sums = [0.0] * 3
        for lanes, chunk in corners(tile):
            masks = [chunk == h for h in range(1, 5)]
            for d in range(3):
                value = 0.0
                for h in range(1, 5):
                    value = jnp.where(masks[h - 1], take(nodes[6 * d + h], lanes), value)
                sums[d] = sums[d] + value
        sweeps[rows8(tile), :] = dot3(normal_of(tile), sums)

    def outer_sweep(tile):
        sums = [0.0] * 3
        for lanes, chunk in corners(tile):
            below, above = chunk == 0, chunk == 5
            for d in range(3):
                value = jnp.where(below, take(nodes[6 * d], lanes), 0.0)
                sums[d] = sums[d] + jnp.where(above, take(nodes[6 * d + 5], lanes), value)
        total = sweeps[rows8(tile), :] + dot3(normal_of(tile), sums)
        sweeps[rows8(tile), :] = (0.25 * STEP_SIZE) * total

    def inner_tiles(t, _):
        for i in range(5):
            inner_sweep(5 * t + i)
        return 0

    lax.fori_loop(0, HOLD, inner_tiles, 0)
    if remote:

        @pl.when(late == 1)
        def _():
            for half in range(2):
                exchange(HELD, half).start()

    lax.fori_loop(HOLD, TILES // 5, inner_tiles, 0)

    for side in range(2):
        where = split_cells(inner_cells[pl.ds(side, 8, stride=2), :])
        normal = normal_of(0)
        out = rebuild(table, where, [-x for x in normal] if side else normal)
        for v in range(5):
            inner_sides[side, v] = out[v]


    for side in range(2):
        if remote:
            receives = has_nxt if side else has_prv

            @pl.when(receives == 1)
            def _(side=side):
                halo_copy(side).wait_recv()

        else:
            halo_copy(side).wait()
        for d in range(3):
            nodes[6 * d + 5 * side] = jnp.broadcast_to(halo[side, d : d + 1, :], (8, CB))
    if remote:
        for what in range(3):
            cross(what)

    for tile in [0] + [1 + RT * FLUX_ORDER[0] + t for t in range(RT)]:
        outer_sweep(tile)

    total[...] = jnp.zeros_like(total)
    split[...] = jnp.zeros_like(split)

    normal = normal_of(0)
    sweep = sweeps[0:8, :]
    left_cells = inner_cells[pl.ds(0, 8, stride=2), :]
    right_cells = inner_cells[pl.ds(1, 8, stride=2), :]
    left = [inner_sides[0, v] for v in range(5)]
    right = [inner_sides[1, v] for v in range(5)]
    flux = roe_flux(left, right, normal, sweep)
    scatter([-x for x in flux] + [sweep], left_cells, split.at[0], total)
    scatter(flux + [-sweep], right_cells, split.at[1], total)

    early_order, late_order = FLUX_ORDER + (HELD, CROSSING), FLUX_ORDER + (CROSSING, HELD)

    def at_place(place):
        if not remote or early_order[place] == late_order[place]:
            return early_order[place]
        return late_order[place] * late + early_order[place] * (1 - late)

    for place in range(ROUNDS):
        index = at_place(place)
        later = at_place(place + 1) if place + 1 < ROUNDS else None
        if remote and place == 1:
            cross(3)

        def flux_tile(pair, half, index=index):
            tile = 1 + RT * index + 2 * pair + half
            ours = [own[2 * index + pair, v, rows8(half), :] for v in range(5)]
            other = [theirs[2 * index + pair, v, rows8(half), :] for v in range(5)]
            sweep = sweeps[rows8(tile), :]
            flux = roe_flux(ours, other, normal_of(tile), sweep)
            scatter([-x for x in flux] + [sweep], cells_of(index, 2 * pair + half), split.at[half], total)

        def flux_pair(pair, _, later=later):
            if later is not None:
                for i in range(2):
                    outer_sweep(1 + RT * later + 2 * pair + i)
            flux_tile(pair, 0)
            flux_tile(pair, 1)
            return 0

        if early_order[place] in (HELD, CROSSING):
            for pair in range(2):
                if remote:
                    for side, order in ((0, early_order), (1, late_order)):

                        @pl.when(late == side)
                        def _(index=order[place], pair=pair):
                            exchange(index, pair).wait()

                else:
                    exchange(index, pair).wait()
                flux_pair(pair, 0)
        else:
            exchange(index).wait()
            lax.fori_loop(0, RT // 2, flux_pair, 0)

    if remote:

        @pl.when(has_nxt == 1)
        def _():
            halo_copy(0).wait_send()

        @pl.when(has_prv == 1)
        def _():
            halo_copy(1).wait_send()


def finish(total, state, volume, counts, content, new_volume):
    live = jnp.broadcast_to(counts[...], (8, CB))
    for h in range(4):
        on = live > h
        sums = total[h * 16 : h * 16 + 6, :] + total[h * 16 + 6 : h * 16 + 12, :]
        room = volume[h : h + 1, :]
        content[:, h, :] = room * state[:, h, :] + jnp.where(on[0:5], STEP_SIZE * sums[0:5, :], 0.0)
        new_volume[h : h + 1, :] = room + jnp.where(on[0:1], sums[5:6, :], 0.0)


def section(remote, state, grad, adjacency, node_vel, face_normal, face_nodes, inner_cells, iface_cells, volume, counts):
    vmem = pl.BlockSpec(memory_space=pltpu.VMEM)
    hbm = pl.BlockSpec(memory_space=pltpu.HBM)
    params = dict(vmem_limit_bytes=VMEM_LIMIT)
    if remote:
        params.update(collective_id=0, has_side_effects=True)
    inputs = (state, grad, adjacency, node_vel, face_normal, face_nodes, inner_cells, iface_cells)
    total = pl.pallas_call(
        functools.partial(kernel, remote),
        out_shape=jax.ShapeDtypeStruct((64, CB), F32),
        in_specs=[hbm] * 8,
        out_specs=vmem,
        scratch_shapes=[
            *(pltpu.VMEM(x.shape, x.dtype) for x in inputs),
            pltpu.VMEM((80, 8, CB), F32),
            pltpu.VMEM((18, 8, CB), F32),
            pltpu.VMEM((2 * ROUNDS, 5, RT * 4, CB), F32),
            pltpu.VMEM((2 * ROUNDS, 5, RT * 4, CB), F32),
            pltpu.VMEM((TILES * 8, CB), F32),
            pltpu.VMEM((2, 3, HN), F32),
            pltpu.VMEM((2, 8 * RS, CB), F32),
            pltpu.SemaphoreType.DMA((2 * ROUNDS,)),
            pltpu.SemaphoreType.DMA((2 * ROUNDS,)),
            pltpu.SemaphoreType.DMA((2,)),
            pltpu.SemaphoreType.DMA((2,)),
            pltpu.SemaphoreType.DMA((7,)),
            pltpu.SemaphoreType.DMA((NB,)),
            pltpu.SemaphoreType.REGULAR((3,)),
            pltpu.VMEM((2, 5, 8, CB), F32),
        ],
        compiler_params=pltpu.CompilerParams(**params),
    )(*inputs)
    return pl.pallas_call(
        finish,
        out_shape=(
            jax.ShapeDtypeStruct((5, NB, CB), F32),
            jax.ShapeDtypeStruct((NB, CB), F32),
        ),
        in_specs=[vmem] * 4,
        out_specs=(vmem, vmem),
    )(total, state, volume, counts)


def by_chunk(rows):
    count, length = rows.shape
    return rows.reshape(count, length // CB, CB).swapaxes(0, 1).reshape(count * length // CB, CB)


def shards(
    state,
    grad_op,
    adjacency,
    node_vel,
    face_normal,
    face_nodes,
    inner_cells,
    iface_cells,
    cell_volume,
    block_counts,
):
    content, new_volume = section(
        True,
        state.reshape(5, NB, CB),
        grad_op.reshape(NB, K, CB, 3 * CB),
        jnp.swapaxes(adjacency, 2, 3).reshape(K, 1, NB),
        node_vel.reshape(3, NB, CB),
        face_normal.reshape(3, TILES * 8, CB),
        by_chunk(face_nodes[0, 0]),
        by_chunk(inner_cells[0, 0]),
        iface_cells.reshape(ROUNDS, RT * 8, CB),
        cell_volume.reshape(NB, CB),
        block_counts,
    )
    return (content.reshape(1, 1, 5, NN), new_volume.reshape(1, 1, NN))


def solution(mesh):
    return jax.shard_map(
        shards,
        mesh=mesh,
        in_specs=(
            P("zone", "dom", None, None),
            P("zone", "dom", None, None, None, None),
            P("zone", "dom", None, None),
            P("zone", "dom", None, None),
            P("zone", "dom", None, None),
            P("zone", "dom", None, None),
            P("zone", "dom", None, None),
            P("zone", "dom", None, None),
            P("zone", "dom", None),
            P("zone", "dom"),
        ),
        out_specs=(P("zone", "dom", None, None), P("zone", "dom", None)),
        check_vma=False,
    )
```

```python
import functools

import jax
import jax.numpy as jnp
from jax import lax
from jax.experimental import pallas as pl
from jax.experimental.pallas import tpu as pltpu
from jax.sharding import PartitionSpec as P

CB = 128
NB = 4
K = 3
ROUNDS = 6
HN = 128
NN = 512
RT = 4
TILES = 25
RS = 24

STEP_SIZE = 0.25
RECON_GAIN = 0.2
GAMMA_LESS = 0.4

LATE_ORDER = (2, 5, 3, 0, 4, 1)
EARLY_ORDER = (1, 4, 5, 3, 0, 2)
FLUX_ORDER = (0, 3, 5, 4)

REST_AFTER = 1
CROSSING = 2
HELD = 1
HOLD = 3
VMEM_LIMIT = 60 << 20

F32 = jnp.float32
BF16 = jnp.bfloat16


def take(row, lanes):
    return jnp.take_along_axis(row, lanes, axis=1, mode="promise_in_bounds")


def rows8(tile):
    return pl.ds(pl.multiple_of(tile * 8, 8), 8)


def split_cells(cells):
    return cells & 127, (cells & 128) != 0, (cells & 256) != 0


def pick(table, first, where):
    lanes, odd, upper = where
    low = jnp.where(odd, take(table[first + 1], lanes), take(table[first], lanes))
    high = jnp.where(odd, take(table[first + 3], lanes), take(table[first + 2], lanes))
    return jnp.where(upper, high, low)


def rebuild(table, where, normal):
    cons = [pick(table, 4 * v, where) for v in range(5)]
    delta = []
    for v in range(5):
        parts = [pick(table, 20 + 4 * (3 * v + d), where) * normal[d] for d in range(3)]
        delta.append(parts[0] + parts[1] + parts[2])
    per_dens = 1.0 / cons[0]
    gain = RECON_GAIN * cons[0]
    out = [cons[0] + gain * jnp.tanh(delta[0] * per_dens)]
    for v in range(1, 4):
        out.append(cons[v] + gain * jnp.tanh(delta[v] * per_dens))
    out.append(cons[4] + RECON_GAIN * cons[4] * jnp.tanh(delta[4] / cons[4]))
    return out


def dot3(a, b):
    return a[0] * b[0] + a[1] * b[1] + a[2] * b[2]


def side_values(cons, unit):
    per_dens = 1.0 / cons[0]
    vel = [cons[i] * per_dens for i in (1, 2, 3)]
    pres = GAMMA_LESS * (cons[4] - 0.5 * dot3(cons[1:4], vel))
    enth = (cons[4] + pres) * per_dens
    return vel, pres, enth, dot3(vel, unit)


def roe_flux(left, right, normal, sweep):
    area_sq = dot3(normal, normal)
    per_area = lax.rsqrt(area_sq)
    area = area_sq * per_area
    unit = [x * per_area for x in normal]
    grid = sweep * per_area * (1.0 / STEP_SIZE)
    vel_l, pres_l, enth_l, q_l = side_values(left, unit)
    vel_r, pres_r, enth_r, q_r = side_values(right, unit)
    root_l = jnp.sqrt(left[0])
    root_r = jnp.sqrt(right[0])
    per_sum = 1.0 / (root_l + root_r)
    a = root_l * per_sum
    b = root_r * per_sum
    vel = [a * x + b * y for x, y in zip(vel_l, vel_r)]
    enth = a * enth_l + b * enth_r
    dens = root_l * root_r
    q = dot3(vel, unit)
    kinetic = 0.5 * dot3(vel, vel)
    c_sq = GAMMA_LESS * (enth - kinetic)
    c = jnp.sqrt(c_sq)
    per_c_sq = 1.0 / c_sq
    d_pres = pres_r - pres_l
    d_dens = right[0] - left[0]
    d_vel = [y - x for x, y in zip(vel_l, vel_r)]
    d_q = dot3(d_vel, unit)
    fix = 0.01 * c_sq
    rel = q - grid
    slow = rel - c
    fast = rel + c
    wave_slow = jnp.sqrt(slow * slow + fix)
    wave_mid = jnp.sqrt(rel * rel + fix)
    wave_fast = jnp.sqrt(fast * fast + fix)
    half = 0.5 * per_c_sq
    cross = dens * c * d_q
    part_slow = wave_slow * ((d_pres - cross) * half)
    part_fast = wave_fast * ((d_pres + cross) * half)
    part_mid = wave_mid * (d_dens - d_pres * per_c_sq)
    shear = wave_mid * dens
    both = part_slow + part_fast
    total = both + part_mid
    diff = c * (part_fast - part_slow)
    move_l = q_l - grid
    move_r = q_r - grid
    along = pres_l + pres_r - diff + shear * d_q
    out = [left[0] * move_l + right[0] * move_r - total]
    for i in range(3):
        out.append(
            left[i + 1] * move_l
            + right[i + 1] * move_r
            + along * unit[i]
            - total * vel[i]
            - shear * d_vel[i]
        )
    out.append(
        left[4] * move_l
        + right[4] * move_r
        + pres_l * q_l
        + pres_r * q_r
        - both * enth
        - diff * q
        - part_mid * kinetic
        - shear * (dot3(vel, d_vel) - q * d_q)
    )
    scale = 0.5 * area
    return [scale * x for x in out]


def scatter(terms, where_cells, split, total):
    for v, x in enumerate(terms):
        upper = x.astype(BF16).astype(F32)
        split[pl.ds(v, 8, stride=RS), :] = upper
        split[pl.ds(v + 6, 8, stride=RS), :] = x - upper
    lanes = (where_cells & 127).astype(F32)
    chunk = (where_cells >> 7).astype(F32)
    slot = lax.broadcasted_iota(jnp.int32, (CB, CB), 0).astype(F32).astype(BF16)
    one, zero = jnp.ones((), BF16), jnp.zeros((), BF16)
    result = None
    for s in range(0, 8, 2):
        left, right = [], []
        for i in (s, s + 1):
            rows = split[i * RS : i * RS + 16, :].astype(BF16)
            home = jnp.broadcast_to(chunk[i : i + 1, :], (16, CB)).astype(BF16)
            left.append(jnp.concatenate([jnp.where(home == h, rows, zero) for h in range(4)], axis=0))
            at = jnp.broadcast_to(lanes[i : i + 1, :], (CB, CB)).astype(BF16)
            right.append(jnp.where(at == slot, one, zero))
        left, right = jnp.concatenate(left, axis=1), jnp.concatenate(right, axis=1)
        part = lax.dot_general(right, left, (((1,), (1,)), ((), ())), preferred_element_type=F32)
        result = part if result is None else result + part
    total[...] += result


def kernel(
    remote,
    state_hbm,
    grad_hbm,
    adjacency_hbm,
    node_vel_hbm,
    face_normal_hbm,
    face_nodes_hbm,
    inner_cells_hbm,
    iface_cells_hbm,
    total,
    state,
    grad,
    adjacency,
    node_vel,
    face_normal,
    face_nodes,
    inner_cells,
    iface_cells,
    table,
    nodes,
    own,
    theirs,
    sweeps,
    halo,
    split,
    send_sem,
    recv_sem,
    halo_send,
    halo_recv,
    stage_sem,
    grad_sem,
    ready,
    inner_sides,
):
    def stage(source, target, sem):
        copy = pltpu.make_async_copy(source, target, sem)
        copy.start()
        return copy

    halo[...] = jnp.zeros_like(halo)
    staged_state = stage(state_hbm, state, stage_sem.at[0])
    staged_adjacency = stage(adjacency_hbm, adjacency, stage_sem.at[1])
    staged_grad = [stage(grad_hbm.at[b], grad.at[b], grad_sem.at[b]) for b in range(NB)]
    staged_first = [
        stage(iface_cells_hbm, iface_cells, stage_sem.at[2]),
        stage(face_normal_hbm, face_normal, stage_sem.at[3]),
    ]

    def stage_rest():
        return [
            stage(node_vel_hbm, node_vel, stage_sem.at[4]),
            stage(inner_cells_hbm, inner_cells, stage_sem.at[5]),
            stage(face_nodes_hbm, face_nodes, stage_sem.at[6]),
        ]

    if remote:
        zone = lax.axis_index("zone")
        dom = lax.axis_index("dom")
        n_dom = lax.axis_size("dom")
        nxt = lax.rem(dom + 1, n_dom)
        prv = lax.rem(dom + n_dom - 1, n_dom)
        has_nxt = 1 - (dom + 1) // n_dom
        has_prv = 1 - (n_dom - dom) // n_dom

        def flip(at, bit):
            return at + bit * (1 - 2 * ((at // bit) % 2))

        peers = [
            (zone, flip(dom, 1)),
            (zone, flip(dom, 2)),
            (zone, flip(dom, 4)),
            (zone, flip(dom, 8)),
            (flip(zone, 1), dom),
            (zone, flip(dom, 16)),
        ]
        def is_late(at):
            return (at // 4) % 2

        late = is_late(dom)
        early = 1 - late
        late_nxt = is_late(nxt)
        late_prv = is_late(prv)

        def signal(sem, peer):
            pl.semaphore_signal(sem, inc=1, device_id=peer, device_id_type=pl.DeviceIdType.MESH)

        barrier = pltpu.get_barrier_semaphore()
        for index in (4, 1, 0, 3, 5):
            signal(barrier, peers[index])

        @pl.when(early == 1)
        def _():
            signal(barrier, peers[2])

        @pl.when(has_nxt * (early + late_nxt) > 0)
        def _():
            signal(barrier, (zone, nxt))

        @pl.when(has_prv * (early + late_prv) > 0)
        def _():
            signal(barrier, (zone, prv))

    def exchange(index, half=None):
        if half is None:
            at, sem = pl.ds(2 * index, 2), 2 * index
        else:
            at = sem = 2 * index + half
        if remote:
            return pltpu.make_async_remote_copy(
                src_ref=own.at[at],
                dst_ref=theirs.at[at],
                send_sem=send_sem.at[sem],
                recv_sem=recv_sem.at[sem],
                device_id=peers[index],
                device_id_type=pl.DeviceIdType.MESH,
            )
        return pltpu.make_async_copy(own.at[at], theirs.at[at], recv_sem.at[sem])

    def halo_copy(side):
        source = node_vel_hbm.at[:, 3 * (1 - side), :]
        if remote:
            return pltpu.make_async_remote_copy(
                src_ref=source,
                dst_ref=halo.at[side],
                send_sem=halo_send.at[side],
                recv_sem=halo_recv.at[side],
                device_id=(zone, prv if side else nxt),
                device_id_type=pl.DeviceIdType.MESH,
            )
        return pltpu.make_async_copy(source, halo.at[side], halo_recv.at[side])

    def enter():
        meet_nxt = has_nxt * (1 - early * late_nxt)
        meet_prv = has_prv * (1 - early * late_prv)
        pl.semaphore_wait(barrier, 5 + late + meet_nxt + meet_prv)

        @pl.when(late == 1)
        def _():
            signal(ready.at[0], peers[2])

        @pl.when(late * (1 - late_nxt) * has_nxt == 1)
        def _():
            signal(ready.at[1], (zone, nxt))

        @pl.when(late * (1 - late_prv) * has_prv == 1)
        def _():
            signal(ready.at[2], (zone, prv))

        @pl.when(meet_nxt == 1)
        def _():
            halo_copy(0).start()

        @pl.when(meet_prv == 1)
        def _():
            halo_copy(1).start()

    def cross(what):
        if what == 0:

            @pl.when(early * late_nxt * has_nxt == 1)
            def _():
                pl.semaphore_wait(ready.at[2], 1)
                halo_copy(0).start()

        elif what == 1:

            @pl.when(early * late_prv * has_prv == 1)
            def _():
                pl.semaphore_wait(ready.at[1], 1)
                halo_copy(1).start()

        else:
            mixed = late_nxt * has_nxt + late_prv * has_prv

            @pl.when(early * (mixed if what == 2 else 1 - mixed) == 1)
            def _():
                pl.semaphore_wait(ready.at[0], 1)
                for half in range(2):
                    exchange(CROSSING, half).start()

    staged_state.wait()
    staged_adjacency.wait()
    for v in range(5):
        for h in range(4):
            table[4 * v + h] = jnp.broadcast_to(state[v, h : h + 1, :], (8, CB))
    for b in range(NB):
        sums = None
        staged_grad[b].wait()
        if b == REST_AFTER:
            staged_late = stage_rest()
            if remote:
                pl.when(late == 1)(enter)
        for k in range(K):
            near = jnp.broadcast_to(adjacency[k, :, b : b + 1], (5, CB))
            block = state[:, 0, :]
            for other in range(1, NB):
                block = jnp.where(near == other, state[:, other, :], block)
            part = jnp.dot(block.astype(BF16), grad[b, k], preferred_element_type=F32)
            sums = part if sums is None else sums + part
        for v in range(5):
            for d in range(3):
                table[20 + 4 * (3 * v + d) + b] = jnp.broadcast_to(
                    sums[v : v + 1, d * CB : (d + 1) * CB], (8, CB)
                )

    def normal_of(tile):
        return [face_normal[d, rows8(tile), :] for d in range(3)]

    def cells_of(index, t):
        return iface_cells[index, rows8(t), :]

    if remote:
        pl.when(early == 1)(enter)
    else:
        for side in range(2):
            halo_copy(side).start()

    for copy in staged_first:
        copy.wait()

    for place in range(ROUNDS):
        late_index, early_index = LATE_ORDER[place], EARLY_ORDER[place]
        index = late_index * late + early_index * (1 - late) if remote else late_index
        for half in range(2):
            for t in range(2):
                tile = 2 * half + t
                where = split_cells(cells_of(index, tile))
                out = rebuild(table, where, normal_of(1 + RT * index + tile))
                for v in range(5):
                    own[2 * index + half, v, rows8(t), :] = out[v]
            if late_index == CROSSING:
                if remote:

                    @pl.when(late == 1)
                    def _(half=half):
                        exchange(CROSSING, half).start()

                else:
                    exchange(CROSSING, half).start()
        if remote:
            if late_index not in (CROSSING, HELD):

                @pl.when(late == 1)
                def _(index=late_index):
                    exchange(index).start()

            if early_index != CROSSING:

                @pl.when(late == 0)
                def _(index=early_index):
                    for half in (0, 1) if index == HELD else (None,):
                        exchange(index, half).start()

        elif late_index == HELD:
            for half in range(2):
                exchange(HELD, half).start()
        elif late_index != CROSSING:
            exchange(late_index).start()

    for copy in staged_late:
        copy.wait()

    for d in range(3):
        for h in range(4):
            nodes[6 * d + 1 + h] = jnp.broadcast_to(node_vel[d, h : h + 1, :], (8, CB))

    def corners(tile):
        for corner in range(4):
            at = face_nodes[pl.ds(tile * 32 + corner, 8, stride=4), :]
            yield at & 127, at >> 7

    def inner_sweep(tile):
        sums = [0.0] * 3
        for lanes, chunk in corners(tile):
            masks = [chunk == h for h in range(1, 5)]
            for d in range(3):
                value = 0.0
                for h in range(1, 5):
                    value = jnp.where(masks[h - 1], take(nodes[6 * d + h], lanes), value)
                sums[d] = sums[d] + value
        sweeps[rows8(tile), :] = dot3(normal_of(tile), sums)

    def outer_sweep(tile):
        sums = [0.0] * 3
        for lanes, chunk in corners(tile):
            below, above = chunk == 0, chunk == 5
            for d in range(3):
                value = jnp.where(below, take(nodes[6 * d], lanes), 0.0)
                sums[d] = sums[d] + jnp.where(above, take(nodes[6 * d + 5], lanes), value)
        total = sweeps[rows8(tile), :] + dot3(normal_of(tile), sums)
        sweeps[rows8(tile), :] = (0.25 * STEP_SIZE) * total

    def inner_tiles(t, _):
        for i in range(5):
            inner_sweep(5 * t + i)
        return 0

    lax.fori_loop(0, HOLD, inner_tiles, 0)
    if remote:

        @pl.when(late == 1)
        def _():
            for half in range(2):
                exchange(HELD, half).start()

    lax.fori_loop(HOLD, TILES // 5, inner_tiles, 0)

    for side in range(2):
        where = split_cells(inner_cells[pl.ds(side, 8, stride=2), :])
        normal = normal_of(0)
        out = rebuild(table, where, [-x for x in normal] if side else normal)
        for v in range(5):
            inner_sides[side, v] = out[v]


    for side in range(2):
        if remote:
            receives = has_nxt if side else has_prv

            @pl.when(receives == 1)
            def _(side=side):
                halo_copy(side).wait_recv()

        else:
            halo_copy(side).wait()
        for d in range(3):
            nodes[6 * d + 5 * side] = jnp.broadcast_to(halo[side, d : d + 1, :], (8, CB))
    if remote:
        for what in range(3):
            cross(what)

    for tile in [0] + [1 + RT * FLUX_ORDER[0] + t for t in range(RT)]:
        outer_sweep(tile)

    total[...] = jnp.zeros_like(total)
    split[...] = jnp.zeros_like(split)

    normal = normal_of(0)
    sweep = sweeps[0:8, :]
    left_cells = inner_cells[pl.ds(0, 8, stride=2), :]
    right_cells = inner_cells[pl.ds(1, 8, stride=2), :]
    left = [inner_sides[0, v] for v in range(5)]
    right = [inner_sides[1, v] for v in range(5)]
    flux = roe_flux(left, right, normal, sweep)
    scatter([-x for x in flux] + [sweep], left_cells, split.at[0], total)
    scatter(flux + [-sweep], right_cells, split.at[1], total)

    early_order, late_order = FLUX_ORDER + (HELD, CROSSING), FLUX_ORDER + (CROSSING, HELD)

    def at_place(place):
        if not remote or early_order[place] == late_order[place]:
            return early_order[place]
        return late_order[place] * late + early_order[place] * (1 - late)

    for place in range(ROUNDS):
        index = at_place(place)
        later = at_place(place + 1) if place + 1 < ROUNDS else None
        if remote and place == 1:
            cross(3)

        def flux_tile(pair, half, index=index):
            tile = 1 + RT * index + 2 * pair + half
            ours = [own[2 * index + pair, v, rows8(half), :] for v in range(5)]
            other = [theirs[2 * index + pair, v, rows8(half), :] for v in range(5)]
            sweep = sweeps[rows8(tile), :]
            flux = roe_flux(ours, other, normal_of(tile), sweep)
            scatter([-x for x in flux] + [sweep], cells_of(index, 2 * pair + half), split.at[half], total)

        def flux_pair(pair, _, later=later):
            if later is not None:
                for i in range(2):
                    outer_sweep(1 + RT * later + 2 * pair + i)
            flux_tile(pair, 0)
            flux_tile(pair, 1)
            return 0

        if early_order[place] in (HELD, CROSSING):
            for pair in range(2):
                if remote:
                    for side, order in ((0, early_order), (1, late_order)):

                        @pl.when(late == side)
                        def _(index=order[place], pair=pair):
                            exchange(index, pair).wait()

                else:
                    exchange(index, pair).wait()
                flux_pair(pair, 0)
        else:
            exchange(index).wait()
            lax.fori_loop(0, RT // 2, flux_pair, 0)

    if remote:

        @pl.when(has_nxt == 1)
        def _():
            halo_copy(0).wait_send()

        @pl.when(has_prv == 1)
        def _():
            halo_copy(1).wait_send()


def finish(total, state, volume, counts, content, new_volume):
    live = jnp.broadcast_to(counts[...], (8, CB))
    flat = total[...].T
    for h in range(4):
        on = live > h
        sums = flat[h * 16 : h * 16 + 6, :] + flat[h * 16 + 6 : h * 16 + 12, :]
        room = volume[h : h + 1, :]
        content[:, h, :] = room * state[:, h, :] + jnp.where(on[0:5], STEP_SIZE * sums[0:5, :], 0.0)
        new_volume[h : h + 1, :] = room + jnp.where(on[0:1], sums[5:6, :], 0.0)


def section(remote, state, grad, adjacency, node_vel, face_normal, face_nodes, inner_cells, iface_cells, volume, counts):
    vmem = pl.BlockSpec(memory_space=pltpu.VMEM)
    hbm = pl.BlockSpec(memory_space=pltpu.HBM)
    params = dict(vmem_limit_bytes=VMEM_LIMIT)
    if remote:
        params.update(collective_id=0, has_side_effects=True)
    inputs = (state, grad, adjacency, node_vel, face_normal, face_nodes, inner_cells, iface_cells)
    total = pl.pallas_call(
        functools.partial(kernel, remote),
        out_shape=jax.ShapeDtypeStruct((CB, 64), F32),
        in_specs=[hbm] * 8,
        out_specs=vmem,
        scratch_shapes=[
            *(pltpu.VMEM(x.shape, x.dtype) for x in inputs),
            pltpu.VMEM((80, 8, CB), F32),
            pltpu.VMEM((18, 8, CB), F32),
            pltpu.VMEM((2 * ROUNDS, 5, RT * 4, CB), F32),
            pltpu.VMEM((2 * ROUNDS, 5, RT * 4, CB), F32),
            pltpu.VMEM((TILES * 8, CB), F32),
            pltpu.VMEM((2, 3, HN), F32),
            pltpu.VMEM((2, 8 * RS, CB), F32),
            pltpu.SemaphoreType.DMA((2 * ROUNDS,)),
            pltpu.SemaphoreType.DMA((2 * ROUNDS,)),
            pltpu.SemaphoreType.DMA((2,)),
            pltpu.SemaphoreType.DMA((2,)),
            pltpu.SemaphoreType.DMA((7,)),
            pltpu.SemaphoreType.DMA((NB,)),
            pltpu.SemaphoreType.REGULAR((3,)),
            pltpu.VMEM((2, 5, 8, CB), F32),
        ],
        compiler_params=pltpu.CompilerParams(**params),
    )(*inputs)
    return pl.pallas_call(
        finish,
        out_shape=(
            jax.ShapeDtypeStruct((5, NB, CB), F32),
            jax.ShapeDtypeStruct((NB, CB), F32),
        ),
        in_specs=[vmem] * 4,
        out_specs=(vmem, vmem),
    )(total, state, volume, counts)


def by_chunk(rows):
    count, length = rows.shape
    return rows.reshape(count, length // CB, CB).swapaxes(0, 1).reshape(count * length // CB, CB)


def shards(
    state,
    grad_op,
    adjacency,
    node_vel,
    face_normal,
    face_nodes,
    inner_cells,
    iface_cells,
    cell_volume,
    block_counts,
):
    content, new_volume = section(
        True,
        state.reshape(5, NB, CB),
        grad_op.reshape(NB, K, CB, 3 * CB),
        jnp.swapaxes(adjacency, 2, 3).reshape(K, 1, NB),
        node_vel.reshape(3, NB, CB),
        face_normal.reshape(3, TILES * 8, CB),
        by_chunk(face_nodes[0, 0]),
        by_chunk(inner_cells[0, 0]),
        iface_cells.reshape(ROUNDS, RT * 8, CB),
        cell_volume.reshape(NB, CB),
        block_counts,
    )
    return (content.reshape(1, 1, 5, NN), new_volume.reshape(1, 1, NN))


def solution(mesh):
    return jax.shard_map(
        shards,
        mesh=mesh,
        in_specs=(
            P("zone", "dom", None, None),
            P("zone", "dom", None, None, None, None),
            P("zone", "dom", None, None),
            P("zone", "dom", None, None),
            P("zone", "dom", None, None),
            P("zone", "dom", None, None),
            P("zone", "dom", None, None),
            P("zone", "dom", None, None),
            P("zone", "dom", None),
            P("zone", "dom"),
        ),
        out_specs=(P("zone", "dom", None, None), P("zone", "dom", None)),
        check_vma=False,
    )
```
